32 devices in a mesh: cuts: 4 (over y, core), rows: 8 (over z, x).
Axes of the slice: x: 2, y: 2, z: 4, core: 2. Of those that a mesh axis runs over, the one named last changes fastest.
Arguments:
- upstream_loss_derivative: float32 [4, 2, 1, 256, 256], P('cuts', None, None, 'rows'), may hold values from -6 to 6
- estimated_slice_image: float32 [4, 2, 1, 256, 256], P('cuts', None, None, 'rows'), may hold values from -6 to 6
- receiver_profile_maps: float32 [4, 8, 2, 256, 256], P('cuts', None, None, 'rows'), may hold values from -1.5 to 1.5
- measured_fourier_data: float32 [4, 8, 2, 1, 256, 256], P('cuts', None, None, None, 'rows'), may hold values from -6 to 6
- acquisition_choice_odds: float32 [1, 256, 256], P(None, 'rows'), may hold values from -6 to 6
- sigmoid_steepness: float32 [1], replicated, may hold values from 0.5 to 2
Outputs:
- adjoint_field: float32 [4, 2, 1, 256, 256], P('cuts', None, None, 'rows')
- logit_gradient_output: float32 [1, 256, 256], P(None, 'rows')
The draws below stay inside these ranges and needn't reach their ends.
All inputs are finite; a program needn't handle non-finite values.
Results may differ from the reference program's by a relative error of at most 0.0001.
Values sent between devices are 32-bit elements; how exact they have to be, the bound alone decides.
No kernel may reach another device: no remote copies, remote signals or barrier semaphores. Data moves between devices by JAX's collectives and lax.ppermute only.
A program may use at most 64 MiB of HBM per device.

```python
import jax
import jax.numpy as jnp
from jax import lax

NX = 256
NY = 256
COILS = 8
FR = 1
ITERS = 3
SLICES = 4


def steps_of(own_key, extent, cuts, low, high):
    factor_of = 1.0
    for position, parts in cuts:
        steps = jax.random.uniform(jax.random.fold_in(jax.random.fold_in(own_key, 6), position), (parts,), jnp.float32, low / len(cuts), high / len(cuts))
        factor_of = factor_of * jnp.repeat(jnp.exp(steps), extent[position] // parts).reshape((-1,) + (1,) * (len(extent) - 1 - position))
    return factor_of


def scatter_about(stream_key, dims, width, most, shards=(), kind=jnp.bfloat16):
    gain = steps_of(stream_key, dims, shards, -0.22, 0.18) if shards else 1.0
    array = jax.random.normal(stream_key, dims, jnp.float32) * width * gain
    return jnp.minimum(jnp.maximum(array, -most), most).astype(kind)


def setup_inputs(seed: int = 0) -> dict:
    streams_of = jax.random.split(jax.random.key(seed), 7)
    return {
        "upstream_loss_derivative": scatter_about(streams_of[0], (SLICES, 2, FR, NX, NY), 1.0, 6.0, ((0, 4), (3, 8)), jnp.float32),
        "estimated_slice_image": scatter_about(streams_of[1], (SLICES, 2, FR, NX, NY), 1.0, 6.0, ((0, 4), (3, 8)), jnp.float32),
        "receiver_profile_maps": scatter_about(streams_of[2], (SLICES, COILS, 2, NX, NY), 0.25, 1.5, ((0, 4), (3, 8)), jnp.float32),
        "measured_fourier_data": scatter_about(streams_of[3], (SLICES, COILS, 2, FR, NY, NX), 1.0, 6.0, ((0, 4), (4, 8)), jnp.float32),
        "acquisition_choice_odds": scatter_about(streams_of[4], (FR, NY, NX), 1.5, 6.0, ((1, 8),), jnp.float32),
        "sigmoid_steepness": jnp.clip(jax.random.uniform(streams_of[5], (1,), jnp.float32, 0.5, 2.0), 0.5, 2.0),
    }


DAMPING = 0.1


def reference(upstream_loss_derivative, estimated_slice_image, receiver_profile_maps, measured_fourier_data, acquisition_choice_odds, sigmoid_steepness):
    temporary_holder = sigmoid_steepness[0]
    weights = jax.nn.sigmoid(temporary_holder * acquisition_choice_odds)

    def solve_slice(packed):
        cot_slice, recon_slice, coil_slice, data_slice = packed
        sensitivity = lax.complex(coil_slice[:, 0], coil_slice[:, 1])[:, None]

        def forward(field):
            spectrum = jnp.fft.fft2(sensitivity * field[None], axes=(-2, -1), norm="ortho")
            return jnp.swapaxes(spectrum, -1, -2)

        def adjoint(spectrum):
            per_coil_pictures = jnp.fft.ifft2(jnp.swapaxes(spectrum, -1, -2), axes=(-2, -1), norm="ortho")
            return jnp.sum(jnp.conj(sensitivity) * per_coil_pictures, axis=0)

        def normal(field):
            return adjoint(weights * forward(field)) + DAMPING * field

        def inner(first, second):
            return jnp.sum(jnp.real(jnp.conj(first) * second))

        right_side = lax.complex(cot_slice[0], cot_slice[1])
        solution = jnp.zeros_like(right_side)
        residual = right_side
        direction = right_side
        norm_now = inner(residual, residual)
        for iteration in range(ITERS):
            image = normal(direction)
            alpha = norm_now / inner(direction, image)
            solution = solution + alpha * direction
            residual = residual - alpha * image
            norm_next = inner(residual, residual)
            direction = residual + (norm_next / norm_now) * direction
            norm_now = norm_next
        spec_solution = forward(solution)
        spec_recon = forward(lax.complex(recon_slice[0], recon_slice[1]))
        measured = lax.complex(data_slice[:, 0], data_slice[:, 1])
        term = jnp.sum(jnp.real(jnp.conj(spec_solution) * (measured - spec_recon)), axis=0)
        return jnp.stack([jnp.real(solution), jnp.imag(solution)]), term

    adjoint_field, terms = lax.map(solve_slice, (upstream_loss_derivative, estimated_slice_image, receiver_profile_maps, measured_fourier_data))
    logit_gradient_output = temporary_holder * weights * (1.0 - weights) * jnp.sum(terms, axis=0) / SLICES
    return adjoint_field, logit_gradient_output
```

```python
import functools
import math

import jax
import jax.numpy as jnp
import ml_dtypes
import numpy as np
from jax import lax
from jax.experimental import pallas as pl
from jax.experimental.pallas import tpu as pltpu
from jax.sharding import PartitionSpec as P

ITERS = 3
DAMPING = 0.1
F32 = jnp.float32
BF16 = jnp.bfloat16
BOTH = ("cuts", "rows")


def host_split(table):
    high = table.astype(np.float32).astype(ml_dtypes.bfloat16)
    low = (table - high.astype(np.float64)).astype(ml_dtypes.bfloat16)
    return high, low


def dft_tables(extent):
    position = np.arange(extent)
    angle = (np.outer(position, position) % extent) * (2.0 * math.pi / extent)
    cos = np.cos(angle) / math.sqrt(extent)
    sin = np.sin(angle) / math.sqrt(extent)
    out = [*host_split(cos)]
    for imag in (-sin, sin):
        out += [*host_split(imag - cos), *host_split(cos + imag)]
    return out


def split(values):
    high = values.astype(BF16)
    low = (values - high.astype(F32)).astype(BF16)
    return high, low


def dot(first, second):
    return lax.dot_general(
        first, second, (((1,), (0,)), ((), ())), preferred_element_type=F32
    )


def by_right(values, high, low):
    vh, vl = split(values)
    return dot(vh, high) + dot(vl, high) + dot(vh, low)


def by_left(values, high, low):
    vh, vl = split(values)
    return dot(high, vh) + dot(high, vl) + dot(low, vh)


def complex_product(multiply, real, imag, t):
    shared = multiply(real + imag, t[0][...], t[1][...])
    cross_real = multiply(real, t[2][...], t[3][...])
    cross_imag = multiply(imag, t[4][...], t[5][...])
    return shared - cross_imag, shared + cross_real


def pick(tables, inverse):
    return [*tables[:2], *(tables[6:10] if inverse else tables[2:6])]


def to_lanes(values, count):
    rows = values.shape[0] // count
    return jnp.concatenate([values[c * rows : (c + 1) * rows] for c in range(count)], axis=1)


def to_rows(values, count):
    cols = values.shape[1] // count
    return jnp.concatenate([values[:, c * cols : (c + 1) * cols] for c in range(count)], axis=0)


def forward(real, imag, maps, count, tables):
    t = pick(tables, False)
    prod_real = jnp.concatenate(
        [maps[2 * c] * real - maps[2 * c + 1] * imag for c in range(count)], axis=0
    )
    prod_imag = jnp.concatenate(
        [maps[2 * c] * imag + maps[2 * c + 1] * real for c in range(count)], axis=0
    )
    re, im = complex_product(by_right, prod_real, prod_imag, t)
    return complex_product(by_left, to_lanes(re, count), to_lanes(im, count), t)


def adjoint(re, im, maps, count, tables):
    t = pick(tables, True)
    re, im = complex_product(by_left, re, im, t)
    re, im = complex_product(by_right, to_rows(re, count), to_rows(im, count), t)
    rows = re.shape[0] // count
    out_real = out_imag = 0.0
    for c in range(count):
        a, b = re[c * rows : (c + 1) * rows], im[c * rows : (c + 1) * rows]
        sr, si = maps[2 * c], maps[2 * c + 1]
        out_real = out_real + (sr * a + si * b)
        out_imag = out_imag + (sr * b - si * a)
    return out_real, out_imag


def total(values):
    return jnp.sum(jnp.sum(values, axis=0, keepdims=True), axis=1, keepdims=True)


def inner(first, second):
    return total(first[0] * second[0] + first[1] * second[1])


def normal(real, imag, maps, count, tables, wt, spec_ref, part_ref):
    re, im = forward(real, imag, maps, count, tables)
    spec_ref[0], spec_ref[1] = re, im
    wide = jnp.concatenate([wt] * count, axis=1)
    part_ref[0], part_ref[1] = adjoint(re * wide, im * wide, maps, count, tables)


def block_row(position, half, blocks, extent):
    return pl.multiple_of(lax.rem(position + half * (blocks // 2), blocks) * extent, extent)


def first_kernel(blocks, planes, half_ref, steep_ref, other_ref, *refs):
    messages, refs = refs[:blocks], refs[blocks:]
    tables, refs = refs[:10], refs[10:]
    maps, image, wt_ref, spec_ref, part_ref, odds, sems = refs
    half = half_ref[0]
    extent = messages[0].shape[1]
    copies = []
    for k in range(blocks):
        mine = pl.ds(block_row(k, half, blocks, extent), extent)
        theirs = pl.ds(block_row(k, 1 - half, blocks, extent), extent)
        msg = messages[k]
        copies += [
            pltpu.make_async_copy(msg.at[:planes], maps.at[:, mine], sems.at[0, k]),
            pltpu.make_async_copy(msg.at[planes], image.at[half, mine], sems.at[1, k]),
            pltpu.make_async_copy(msg.at[planes + 1], odds.at[mine], sems.at[2, k]),
            pltpu.make_async_copy(
                other_ref.at[pl.ds(k * extent, extent)], image.at[1 - half, theirs], sems.at[3, k]
            ),
        ]
    for copy in copies:
        copy.start()
    for copy in copies:
        copy.wait()
    wt = jax.nn.sigmoid(steep_ref[0] * odds[...]).T
    wt_ref[...] = wt
    normal(image[0], image[1], maps, planes // 2, tables, wt, spec_ref, part_ref)


def second_kernel(image, part, other, maps, wt_ref, *refs):
    tables, refs = refs[:10], refs[10:]
    residual_ref, dir_ref, sc_ref, spec_ref, part_ref = refs
    u = (image[0], image[1])
    q = tuple(part[i] + other[i] + DAMPING * u[i] for i in range(2))
    norm = inner(u, u)
    alpha = norm / inner(u, q)
    r = tuple(u[i] - alpha * q[i] for i in range(2))
    norm_next = inner(r, r)
    p = tuple(r[i] + (norm_next / norm) * u[i] for i in range(2))
    for i in range(2):
        residual_ref[i] = r[i]
        dir_ref[i] = p[i]
    sc_ref[0] = jnp.broadcast_to(alpha, sc_ref.shape[1:])
    sc_ref[1] = jnp.broadcast_to(norm_next, sc_ref.shape[1:])
    normal(p[0], p[1], maps, maps.shape[0] // 2, tables, wt_ref[...], spec_ref, part_ref)


def third_kernel(blocks, planes, half_ref, image, res_ref, dir_ref, sc_in, part, other, maps,
                 wt_ref, spec0, spec1, recon_other, *refs):
    messages, refs = refs[:blocks], refs[blocks:]
    tables, refs = refs[:10], refs[10:]
    sol_ref, p_ref, sc_ref, out_ref, data, recon, sems = refs
    half = half_ref[0]
    extent = messages[0].shape[1]
    copies = []
    for k in range(blocks):
        mine = pl.ds(block_row(k, half, blocks, extent), extent)
        theirs = pl.ds(block_row(k, 1 - half, blocks, extent), extent)
        msg = messages[k]
        copies += [
            pltpu.make_async_copy(msg.at[planes], recon.at[half, mine], sems.at[1, k]),
            pltpu.make_async_copy(
                recon_other.at[pl.ds(k * extent, extent)], recon.at[1 - half, theirs], sems.at[2, k]
            ),
            pltpu.make_async_copy(msg.at[:planes], data.at[:, mine], sems.at[0, k]),
        ]
    for copy in copies:
        copy.start()
    count = planes // 2
    n = image.shape[1]
    alpha0, norm = sc_in[0, :1, :1], sc_in[1, :1, :1]
    p = (dir_ref[0], dir_ref[1])
    q = tuple(part[i] + other[i] + DAMPING * p[i] for i in range(2))
    alpha1 = norm / inner(p, q)
    r = tuple(res_ref[i] - alpha1 * q[i] for i in range(2))
    norm_next = inner(r, r)
    for i in range(2):
        sol_ref[i] = alpha0 * image[i] + alpha1 * p[i]
    p = tuple(r[i] + (norm_next / norm) * p[i] for i in range(2))
    p_ref[0], p_ref[1] = p
    re, im = forward(p[0], p[1], maps, count, tables)
    wide = jnp.concatenate([wt_ref[...]] * count, axis=1)
    energy = total(wide * (re * re + im * im))
    sc_ref[0] = jnp.broadcast_to(norm_next, sc_ref.shape[1:])
    sc_ref[1] = jnp.broadcast_to(inner(p, p), sc_ref.shape[1:])
    for copy in copies:
        copy.wait()
    est_re, est_im = forward(recon[0], recon[1], maps, count, tables)
    known = last = 0.0
    for c in range(count):
        s = slice(c * n, (c + 1) * n)
        diff_re = data[2 * c].T - est_re[:, s]
        diff_im = data[2 * c + 1].T - est_im[:, s]
        sol_re = alpha0 * spec0[0, :, s] + alpha1 * spec1[0, :, s]
        sol_im = alpha0 * spec0[1, :, s] + alpha1 * spec1[1, :, s]
        known = known + (sol_re * diff_re + sol_im * diff_im)
        last = last + (re[:, s] * diff_re + im[:, s] * diff_im)
    out_ref[:n] = known
    out_ref[n : 2 * n] = last
    out_ref[2 * n :] = jnp.broadcast_to(energy, (out_ref.shape[0] - 2 * n, n))


def fourth_kernel(half_ref, mine, other, sol, p_ref, sc, *refs):
    outs, terms = refs[:-1], refs[-1]
    half = half_ref[0]
    n = sol.shape[1]
    extent = outs[0].shape[1]
    energy = mine[2 * n :, :][:1, :1] + other[2 * n :, :][:1, :1] + DAMPING * sc[1, :1, :1]
    alpha = sc[0, :1, :1] / energy
    terms[...] = (
        (mine[:n] + other[:n]) + alpha * (mine[n : 2 * n] + other[n : 2 * n])
    ).T
    for k, out in enumerate(outs):
        rows = pl.ds(pl.multiple_of((half * len(outs) + k) * extent, extent), extent)
        out[0] = sol[0, rows] + alpha * p_ref[0, rows]
        out[1] = sol[1, rows] + alpha * p_ref[1, rows]
        out[2] = terms[rows]


VMEM = pl.BlockSpec(memory_space=pltpu.VMEM)
SMEM = pl.BlockSpec(memory_space=pltpu.SMEM)
ANY = pl.BlockSpec(memory_space=pl.ANY)
PARAMS = pltpu.CompilerParams(vmem_limit_bytes=48 << 20)


def shape(*dims):
    return jax.ShapeDtypeStruct(dims, F32)


def home_row(piece, blocks):
    first = blocks // 4
    return first if piece % 2 == 0 else blocks - 1 - first


def gather_pairs(turn, pieces, blocks):
    pairs = []
    for piece in range(pieces):
        for half in range(2):
            source = piece * blocks + (turn + half * (blocks // 2)) % blocks
            target = (piece - piece % 2 + half) * blocks + home_row(piece, blocks)
            pairs.append((source, target))
    return pairs


def scatter_pairs(turn, pieces, blocks):
    pairs = []
    for piece in range(pieces):
        for half in range(2):
            source = (piece - piece % 2 + half) * blocks + home_row(piece, blocks)
            target = piece * blocks + turn + half * (blocks // 2)
            pairs.append((source, target))
    return pairs


def body(
    upstream_loss_derivative,
    estimated_slice_image,
    receiver_profile_maps,
    measured_fourier_data,
    acquisition_choice_odds,
    sigmoid_steepness,
):
    blocks = lax.axis_size("rows")
    pieces = lax.axis_size("cuts")
    row = lax.axis_index("rows")
    half = lax.rem(lax.axis_index("cuts"), 2).astype(jnp.int32)[None]
    late = (row >= blocks // 2).astype(jnp.int32)
    extent = upstream_loss_derivative.shape[3]
    n = upstream_loss_derivative.shape[4]
    coils = receiver_profile_maps.shape[1]
    planes = coils
    count = coils // 2
    tables = [jnp.asarray(t) for t in dft_tables(n)]
    swap = [(i, i ^ 1) for i in range(pieces)]

    maps = receiver_profile_maps.reshape(2, planes, extent, n)
    data = measured_fourier_data.reshape(2, planes, extent, n)
    upstream = upstream_loss_derivative.reshape(2, 1, extent, n)
    recon = estimated_slice_image.reshape(2, 1, extent, n)
    take = lambda values, i: lax.dynamic_index_in_dim(values, i, 0, keepdims=False)

    def gather(build, after=None):
        sends = [build(late), build(1 - late)]
        if after is not None:
            sends = lax.optimization_barrier((*sends, after))[:2]
        return [
            lax.ppermute(sends[k // (blocks // 2)], BOTH, gather_pairs(k, pieces, blocks))
            for k in range(blocks)
        ]

    first = gather(
        lambda i: jnp.concatenate(
            [take(maps, i), take(upstream, i), acquisition_choice_odds], axis=0
        )
    )
    second = gather(
        lambda i: jnp.concatenate([take(data, i), take(recon, i)], axis=0), first[blocks // 2]
    )
    u_mine = jnp.concatenate([m[planes] for m in first], axis=0)
    u_other = lax.ppermute(u_mine, "cuts", swap)

    image, spectrum = shape(2, n, n), shape(2, n, count * n)
    scalars = shape(2, 8, 128)
    stacked = shape(planes, n, n)
    maps_full, u, wt, spec0, part0 = pl.pallas_call(
        functools.partial(first_kernel, blocks, planes),
        name="first_normal",
        in_specs=[SMEM, SMEM, ANY] + [ANY] * blocks + [VMEM] * 10,
        out_specs=[VMEM] * 5,
        out_shape=[stacked, image, shape(n, n), spectrum, image],
        scratch_shapes=[pltpu.VMEM((n, n), F32), pltpu.SemaphoreType.DMA((4, blocks))],
        compiler_params=PARAMS,
    )(half, sigmoid_steepness, u_other, *first, *tables)
    other0 = lax.ppermute(part0, "cuts", swap)
    res1, dir1, sc1, spec1, part1 = pl.pallas_call(
        second_kernel,
        name="second_normal",
        in_specs=[VMEM] * 15,
        out_specs=[VMEM] * 5,
        out_shape=[image, image, scalars, spectrum, image],
        compiler_params=PARAMS,
    )(u, part0, other0, maps_full, wt, *tables)
    r_mine = jnp.concatenate([m[planes] for m in second], axis=0)
    r_other = lax.ppermute(r_mine, "cuts", swap)
    other1 = lax.ppermute(part1, "cuts", swap)
    sol2, dir2, sc2, mine = pl.pallas_call(
        functools.partial(third_kernel, blocks, planes),
        name="last_spectra",
        in_specs=[SMEM] + [VMEM] * 10 + [ANY] + [ANY] * blocks + [VMEM] * 10,
        out_specs=[VMEM] * 4,
        out_shape=[image, image, scalars, shape(2 * n + 8, n)],
        scratch_shapes=[
            pltpu.VMEM((planes, n, n), F32),
            pltpu.VMEM((2, n, n), F32),
            pltpu.SemaphoreType.DMA((3, blocks)),
        ],
        compiler_params=PARAMS,
    )(half, u, res1, dir1, sc1, part1, other1, maps_full, wt, spec0, spec1, r_other, *second, *tables)
    other = lax.ppermute(mine, "cuts", swap)
    turns = blocks // 2
    outs = pl.pallas_call(
        fourth_kernel,
        name="finish",
        in_specs=[SMEM] + [VMEM] * 5,
        out_specs=[VMEM] * turns,
        out_shape=[shape(3, extent, n)] * turns,
        scratch_shapes=[pltpu.VMEM((n, n), F32)],
        compiler_params=PARAMS,
    )(half, mine, other, sol2, dir2, sc2)
    parts = [
        lax.ppermute(outs[k], BOTH, scatter_pairs(k, pieces, blocks)) for k in range(turns)
    ]
    whole = parts[0]
    for part in parts[1:]:
        whole = whole + part
    term = whole[2]
    step = 1
    while step < pieces:
        term = term + lax.ppermute(term, "cuts", [(i, i ^ step) for i in range(pieces)])
        step *= 2
    steep = sigmoid_steepness[0]
    weights = jax.nn.sigmoid(steep * acquisition_choice_odds)
    slices = upstream_loss_derivative.shape[0] * pieces
    gradient = steep * weights * (1.0 - weights) * term[None] / slices
    return whole[:2].reshape(upstream_loss_derivative.shape), gradient


def solution(mesh):
    return jax.shard_map(
        body,
        mesh=mesh,
        in_specs=(
            P("cuts", None, None, "rows", None),
            P("cuts", None, None, "rows", None),
            P("cuts", None, None, "rows", None),
            P("cuts", None, None, None, "rows", None),
            P(None, "rows", None),
            P(),
        ),
        out_specs=(P("cuts", None, None, "rows", None), P(None, "rows", None)),
        check_vma=False,
    )
```

```python
import functools
import math

import jax
import jax.numpy as jnp
import ml_dtypes
import numpy as np
from jax import lax
from jax.experimental import pallas as pl
from jax.experimental.pallas import tpu as pltpu
from jax.sharding import PartitionSpec as P

ITERS = 3
DAMPING = 0.1
F32 = jnp.float32
BF16 = jnp.bfloat16
BOTH = ("cuts", "rows")


def host_split(table):
    high = table.astype(np.float32).astype(ml_dtypes.bfloat16)
    low = (table - high.astype(np.float64)).astype(ml_dtypes.bfloat16)
    return high, low


def dft_tables(extent):
    position = np.arange(extent)
    angle = (np.outer(position, position) % extent) * (2.0 * math.pi / extent)
    cos = np.cos(angle) / math.sqrt(extent)
    sin = np.sin(angle) / math.sqrt(extent)
    out = [*host_split(cos)]
    for imag in (-sin, sin):
        out += [*host_split(imag - cos), *host_split(cos + imag)]
    return out


def split(values):
    high = values.astype(BF16)
    low = (values - high.astype(F32)).astype(BF16)
    return high, low


def dot(first, second):
    return lax.dot_general(
        first, second, (((1,), (0,)), ((), ())), preferred_element_type=F32
    )


def by_right(values, high, low):
    vh, vl = split(values)
    return dot(vh, high) + dot(vl, high) + dot(vh, low)


def by_left(values, high, low):
    vh, vl = split(values)
    return dot(high, vh) + dot(high, vl) + dot(low, vh)


def complex_product(multiply, real, imag, t):
    shared = multiply(real + imag, t[0][...], t[1][...])
    cross_real = multiply(real, t[2][...], t[3][...])
    cross_imag = multiply(imag, t[4][...], t[5][...])
    return shared - cross_imag, shared + cross_real


def pick(tables, inverse):
    return [*tables[:2], *(tables[6:10] if inverse else tables[2:6])]


def to_lanes(values, count):
    rows = values.shape[0] // count
    return jnp.concatenate([values[c * rows : (c + 1) * rows] for c in range(count)], axis=1)


def to_rows(values, count):
    cols = values.shape[1] // count
    return jnp.concatenate([values[:, c * cols : (c + 1) * cols] for c in range(count)], axis=0)


def forward(real, imag, maps, count, tables):
    t = pick(tables, False)
    prod_real = jnp.concatenate(
        [maps[2 * c] * real - maps[2 * c + 1] * imag for c in range(count)], axis=0
    )
    prod_imag = jnp.concatenate(
        [maps[2 * c] * imag + maps[2 * c + 1] * real for c in range(count)], axis=0
    )
    re, im = complex_product(by_right, prod_real, prod_imag, t)
    return complex_product(by_left, to_lanes(re, count), to_lanes(im, count), t)


def adjoint(re, im, maps, count, tables):
    t = pick(tables, True)
    re, im = complex_product(by_left, re, im, t)
    re, im = complex_product(by_right, to_rows(re, count), to_rows(im, count), t)
    rows = re.shape[0] // count
    out_real = out_imag = 0.0
    for c in range(count):
        a, b = re[c * rows : (c + 1) * rows], im[c * rows : (c + 1) * rows]
        sr, si = maps[2 * c], maps[2 * c + 1]
        out_real = out_real + (sr * a + si * b)
        out_imag = out_imag + (sr * b - si * a)
    return out_real, out_imag


def total(values):
    return jnp.sum(jnp.sum(values, axis=0, keepdims=True), axis=1, keepdims=True)


def inner(first, second):
    return total(first[0] * second[0] + first[1] * second[1])


def normal(real, imag, maps, count, tables, wt, spec_ref, part_ref):
    re, im = forward(real, imag, maps, count, tables)
    spec_ref[0], spec_ref[1] = re, im
    wide = jnp.concatenate([wt] * count, axis=1)
    part_ref[0], part_ref[1] = adjoint(re * wide, im * wide, maps, count, tables)


def block_row(turn, flip, extent):
    return pl.multiple_of(lax.bitwise_xor(jnp.int32(turn), flip) * extent, extent)


def at_home(kernel):
    def guarded(*refs):
        @pl.when(refs[0][1] == 1)
        def _():
            kernel(*refs)

    return guarded


def first_kernel(blocks, planes, info, steep_ref, *refs):
    messages, refs = refs[:blocks], refs[blocks:]
    tables, refs = refs[:10], refs[10:]
    maps, image, wt_ref, spec_ref, part_ref, odds, sems = refs
    extent = messages[0].shape[1]
    copies = []
    for k, msg in enumerate(messages):
        rows = pl.ds(block_row(k, info[0], extent), extent)
        copies += [
            pltpu.make_async_copy(msg.at[:planes], maps.at[:, rows], sems.at[0, k]),
            pltpu.make_async_copy(msg.at[pl.ds(planes, 2)], image.at[:, rows], sems.at[1, k]),
            pltpu.make_async_copy(msg.at[planes + 2], odds.at[rows], sems.at[2, k]),
        ]
    for copy in copies:
        copy.start()
    for copy in copies:
        copy.wait()
    wt = jax.nn.sigmoid(steep_ref[0] * odds[...]).T
    wt_ref[...] = wt
    normal(image[0], image[1], maps, planes // 2, tables, wt, spec_ref, part_ref)


def second_kernel(info, image, part, other, maps, wt_ref, *refs):
    tables, refs = refs[:10], refs[10:]
    residual_ref, dir_ref, sc_ref, spec_ref, part_ref = refs
    u = (image[0], image[1])
    q = tuple(part[i] + other[i] + DAMPING * u[i] for i in range(2))
    norm = inner(u, u)
    alpha = norm / inner(u, q)
    r = tuple(u[i] - alpha * q[i] for i in range(2))
    norm_next = inner(r, r)
    p = tuple(r[i] + (norm_next / norm) * u[i] for i in range(2))
    for i in range(2):
        residual_ref[i] = r[i]
        dir_ref[i] = p[i]
    sc_ref[0] = jnp.broadcast_to(alpha, sc_ref.shape[1:])
    sc_ref[1] = jnp.broadcast_to(norm_next, sc_ref.shape[1:])
    normal(p[0], p[1], maps, maps.shape[0] // 2, tables, wt_ref[...], spec_ref, part_ref)


def third_kernel(blocks, planes, info, image, res_ref, dir_ref, sc_in, part, other, maps,
                 wt_ref, spec0_ref, spec1_ref, *refs):
    messages, refs = refs[:blocks], refs[blocks:]
    tables, refs = refs[:10], refs[10:]
    sol_ref, p_ref, sc_ref, out_ref, data, recon, spec0, spec1, sems = refs
    extent = messages[0].shape[1]
    copies = []
    for k, msg in enumerate(messages):
        rows = pl.ds(block_row(k, info[0], extent), extent)
        copies += [
            pltpu.make_async_copy(msg.at[pl.ds(planes, 2)], recon.at[:, rows], sems.at[1, k]),
            pltpu.make_async_copy(msg.at[:planes], data.at[:, rows], sems.at[0, k]),
        ]
    copies += [
        pltpu.make_async_copy(spec0_ref, spec0, sems.at[2, 0]),
        pltpu.make_async_copy(spec1_ref, spec1, sems.at[2, 1]),
    ]
    for copy in copies:
        copy.start()
    count = planes // 2
    n = image.shape[1]
    alpha0, norm = sc_in[0, :1, :1], sc_in[1, :1, :1]
    p = (dir_ref[0], dir_ref[1])
    q = tuple(part[i] + other[i] + DAMPING * p[i] for i in range(2))
    alpha1 = norm / inner(p, q)
    r = tuple(res_ref[i] - alpha1 * q[i] for i in range(2))
    norm_next = inner(r, r)
    for i in range(2):
        sol_ref[i] = alpha0 * image[i] + alpha1 * p[i]
    p = tuple(r[i] + (norm_next / norm) * p[i] for i in range(2))
    p_ref[0], p_ref[1] = p
    re, im = forward(p[0], p[1], maps, count, tables)
    wide = jnp.concatenate([wt_ref[...]] * count, axis=1)
    energy = total(wide * (re * re + im * im))
    sc_ref[0] = jnp.broadcast_to(norm_next, sc_ref.shape[1:])
    sc_ref[1] = jnp.broadcast_to(inner(p, p), sc_ref.shape[1:])
    for copy in copies:
        copy.wait()
    est_re, est_im = forward(recon[0], recon[1], maps, count, tables)
    known = last = 0.0
    for c in range(count):
        s = slice(c * n, (c + 1) * n)
        diff_re = data[2 * c].T - est_re[:, s]
        diff_im = data[2 * c + 1].T - est_im[:, s]
        sol_re = alpha0 * spec0[0, :, s] + alpha1 * spec1[0, :, s]
        sol_im = alpha0 * spec0[1, :, s] + alpha1 * spec1[1, :, s]
        known = known + (sol_re * diff_re + sol_im * diff_im)
        last = last + (re[:, s] * diff_re + im[:, s] * diff_im)
    out_ref[:n] = known
    out_ref[n : 2 * n] = last
    out_ref[2 * n :] = jnp.broadcast_to(energy, (out_ref.shape[0] - 2 * n, n))


def fourth_kernel(info, mine, other, sol, p_ref, sc, *refs):
    outs, terms = refs[:-1], refs[-1]
    half = info[2]
    n = sol.shape[1]
    extent = outs[0].shape[1]
    energy = mine[2 * n :, :][:1, :1] + other[2 * n :, :][:1, :1] + DAMPING * sc[1, :1, :1]
    alpha = sc[0, :1, :1] / energy
    terms[...] = (
        (mine[:n] + other[:n]) + alpha * (mine[n : 2 * n] + other[n : 2 * n])
    ).T
    for k, out in enumerate(outs):
        rows = pl.ds(pl.multiple_of((half * len(outs) + k) * extent, extent), extent)
        out[0] = sol[0, rows] + alpha * p_ref[0, rows]
        out[1] = sol[1, rows] + alpha * p_ref[1, rows]
        out[2] = terms[rows]


VMEM = pl.BlockSpec(memory_space=pltpu.VMEM)
SMEM = pl.BlockSpec(memory_space=pltpu.SMEM)
ANY = pl.BlockSpec(memory_space=pl.ANY)
PARAMS = pltpu.CompilerParams(vmem_limit_bytes=48 << 20)


def shape(*dims):
    return jax.ShapeDtypeStruct(dims, F32)


def home_row(piece, blocks):
    first = blocks // 4
    return first if piece % 2 == 0 else blocks - 1 - first


def gather_pairs(turn, pieces, blocks):
    pairs = []
    for piece in range(pieces):
        for half in range(2):
            block = turn ^ half ^ (blocks // 2 if piece % 2 else 0)
            target = (piece - piece % 2 + half) * blocks + home_row(piece, blocks)
            pairs.append((piece * blocks + block, target))
    return pairs


def scatter_pairs(turn, pieces, blocks):
    pairs = []
    for piece in range(pieces):
        for half in range(2):
            source = (piece - piece % 2 + half) * blocks + home_row(piece, blocks)
            target = piece * blocks + turn + half * (blocks // 2)
            pairs.append((source, target))
    return pairs


def body(
    upstream_loss_derivative,
    estimated_slice_image,
    receiver_profile_maps,
    measured_fourier_data,
    acquisition_choice_odds,
    sigmoid_steepness,
):
    blocks = lax.axis_size("rows")
    pieces = lax.axis_size("cuts")
    row = lax.axis_index("rows")
    half = lax.rem(lax.axis_index("cuts"), 2)
    upper = row >= blocks // 2
    home = (row == home_row(0, blocks)) | (row == home_row(1, blocks))
    flip = jnp.bitwise_xor(half, jnp.where(upper, blocks // 2, 0))
    info = jnp.stack([flip, home.astype(jnp.int32), half]).astype(jnp.int32)
    odd = lax.rem(row, 2)
    extent = upstream_loss_derivative.shape[3]
    n = upstream_loss_derivative.shape[4]
    coils = receiver_profile_maps.shape[1]
    planes = coils
    count = coils // 2
    tables = [jnp.asarray(t) for t in dft_tables(n)]
    swap = [(i, i ^ 1) for i in range(pieces)]

    maps = receiver_profile_maps.reshape(2, planes, extent, n)
    data = measured_fourier_data.reshape(2, planes, extent, n)
    upstream = upstream_loss_derivative.reshape(2, extent, n)
    recon = estimated_slice_image.reshape(2, extent, n)
    take = lambda values, i: lax.dynamic_index_in_dim(values, i, 0, keepdims=False)

    def build(values, *more):
        return [
            jnp.concatenate([take(values, i), *more], axis=0) for i in (odd, 1 - odd)
        ]

    def gather(sends, turns):
        return [
            lax.ppermute(sends[k % 2], BOTH, gather_pairs(k, pieces, blocks)) for k in turns
        ]

    near, far = range(blocks // 2), range(blocks // 2, blocks)
    sends = build(maps, upstream, acquisition_choice_odds)
    first = gather(sends, near) + gather(sends, far)
    sends = build(data, recon)
    sends = lax.optimization_barrier((*sends, *first[: blocks // 2]))[:2]
    second = gather(sends, near)

    image, spectrum = shape(2, n, n), shape(2, n, count * n)
    scalars = shape(2, 8, 128)
    stacked = shape(planes, n, n)
    maps_full, u, wt, spec0, part0 = pl.pallas_call(
        at_home(functools.partial(first_kernel, blocks, planes)),
        name="first_normal",
        in_specs=[SMEM, SMEM] + [ANY] * blocks + [VMEM] * 10,
        out_specs=[VMEM] * 5,
        out_shape=[stacked, image, shape(n, n), spectrum, image],
        scratch_shapes=[pltpu.VMEM((n, n), F32), pltpu.SemaphoreType.DMA((3, blocks))],
        compiler_params=PARAMS,
    )(info, sigmoid_steepness, *first, *tables)
    other0 = lax.ppermute(part0, "cuts", swap)
    sends = lax.optimization_barrier((*sends, part0))[:2]
    second += gather(sends, far)
    res1, dir1, sc1, spec1, part1 = pl.pallas_call(
        at_home(second_kernel),
        name="second_normal",
        in_specs=[SMEM] + [VMEM] * 15,
        out_specs=[VMEM] * 5,
        out_shape=[image, image, scalars, spectrum, image],
        compiler_params=PARAMS,
    )(info, u, part0, other0, maps_full, wt, *tables)
    other1 = lax.ppermute(part1, "cuts", swap)
    sol2, dir2, sc2, mine = pl.pallas_call(
        at_home(functools.partial(third_kernel, blocks, planes)),
        name="last_spectra",
        in_specs=[SMEM] + [VMEM] * 8 + [ANY] * 2 + [ANY] * blocks + [VMEM] * 10,
        out_specs=[VMEM] * 4,
        out_shape=[image, image, scalars, shape(2 * n + 8, n)],
        scratch_shapes=[
            pltpu.VMEM((planes, n, n), F32),
            pltpu.VMEM((2, n, n), F32),
            pltpu.VMEM((2, n, count * n), F32),
            pltpu.VMEM((2, n, count * n), F32),
            pltpu.SemaphoreType.DMA((3, blocks)),
        ],
        compiler_params=PARAMS,
    )(info, u, res1, dir1, sc1, part1, other1, maps_full, wt, spec0, spec1, *second, *tables)
    other = lax.ppermute(mine, "cuts", swap)
    turns = blocks // 2
    outs = pl.pallas_call(
        at_home(fourth_kernel),
        name="finish",
        in_specs=[SMEM] + [VMEM] * 5,
        out_specs=[VMEM] * turns,
        out_shape=[shape(3, extent, n)] * turns,
        scratch_shapes=[pltpu.VMEM((n, n), F32)],
        compiler_params=PARAMS,
    )(info, mine, other, sol2, dir2, sc2)
    parts = [
        lax.ppermute(outs[k], BOTH, scatter_pairs(k, pieces, blocks)) for k in range(turns)
    ]
    whole = parts[0]
    for part in parts[1:]:
        whole = whole + part
    term = whole[2]
    step = 1
    while step < pieces:
        term = term + lax.ppermute(term, "cuts", [(i, i ^ step) for i in range(pieces)])
        step *= 2
    steep = sigmoid_steepness[0]
    weights = jax.nn.sigmoid(steep * acquisition_choice_odds)
    slices = upstream_loss_derivative.shape[0] * pieces
    gradient = steep * weights * (1.0 - weights) * term[None] / slices
    return whole[:2].reshape(upstream_loss_derivative.shape), gradient


def solution(mesh):
    return jax.shard_map(
        body,
        mesh=mesh,
        in_specs=(
            P("cuts", None, None, "rows", None),
            P("cuts", None, None, "rows", None),
            P("cuts", None, None, "rows", None),
            P("cuts", None, None, None, "rows", None),
            P(None, "rows", None),
            P(),
        ),
        out_specs=(P("cuts", None, None, "rows", None), P(None, "rows", None)),
        check_vma=False,
    )
```

```python
import functools
import math

import jax
import jax.numpy as jnp
import ml_dtypes
import numpy as np
from jax import lax
from jax.experimental import pallas as pl
from jax.experimental.pallas import tpu as pltpu
from jax.sharding import PartitionSpec as P


DAMPING = 0.1
F32 = jnp.float32
BF16 = jnp.bfloat16
BOTH = ("cuts", "rows")


def host_split(table):
    high = table.astype(np.float32).astype(ml_dtypes.bfloat16)
    low = (table - high.astype(np.float64)).astype(ml_dtypes.bfloat16)
    return high, low


def dft_tables(extent):
    position = np.arange(extent)
    angle = (np.outer(position, position) % extent) * (2.0 * math.pi / extent)
    cos = np.cos(angle) / math.sqrt(extent)
    sin = np.sin(angle) / math.sqrt(extent)
    out = [*host_split(cos)]
    for imag in (-sin, sin):
        out += [*host_split(imag - cos), *host_split(cos + imag)]
    return out


def split(values):
    high = values.astype(BF16)
    low = (values - high.astype(F32)).astype(BF16)
    return high, low


def dot(first, second):
    return lax.dot_general(
        first, second, (((1,), (0,)), ((), ())), preferred_element_type=F32
    )


def by_right(values, high, low):
    vh, vl = split(values)
    return dot(vh, high) + dot(vl, high) + dot(vh, low)


def by_left(values, high, low):
    vh, vl = split(values)
    return dot(high, vh) + dot(high, vl) + dot(low, vh)


def complex_product(multiply, real, imag, t):
    shared = multiply(real + imag, t[0][...], t[1][...])
    cross_real = multiply(real, t[2][...], t[3][...])
    cross_imag = multiply(imag, t[4][...], t[5][...])
    return shared - cross_imag, shared + cross_real


def pick(tables, inverse):
    return [*tables[:2], *(tables[6:10] if inverse else tables[2:6])]


def to_lanes(values, count):
    rows = values.shape[0] // count
    return jnp.concatenate([values[c * rows : (c + 1) * rows] for c in range(count)], axis=1)


def to_rows(values, count):
    cols = values.shape[1] // count
    return jnp.concatenate([values[:, c * cols : (c + 1) * cols] for c in range(count)], axis=0)


def forward(real, imag, maps, count, tables):
    t = pick(tables, False)
    prod_real = jnp.concatenate(
        [maps[2 * c] * real - maps[2 * c + 1] * imag for c in range(count)], axis=0
    )
    prod_imag = jnp.concatenate(
        [maps[2 * c] * imag + maps[2 * c + 1] * real for c in range(count)], axis=0
    )
    re, im = complex_product(by_right, prod_real, prod_imag, t)
    return complex_product(by_left, to_lanes(re, count), to_lanes(im, count), t)


def adjoint(re, im, maps, count, tables):
    t = pick(tables, True)
    re, im = complex_product(by_left, re, im, t)
    re, im = complex_product(by_right, to_rows(re, count), to_rows(im, count), t)
    rows = re.shape[0] // count
    out_real = out_imag = 0.0
    for c in range(count):
        a, b = re[c * rows : (c + 1) * rows], im[c * rows : (c + 1) * rows]
        sr, si = maps[2 * c], maps[2 * c + 1]
        out_real = out_real + (sr * a + si * b)
        out_imag = out_imag + (sr * b - si * a)
    return out_real, out_imag


def total(values):
    return jnp.sum(jnp.sum(values, axis=0, keepdims=True), axis=1, keepdims=True)


def inner(first, second):
    return total(first[0] * second[0] + first[1] * second[1])


def normal(real, imag, maps, count, tables, wt, spec_ref, part_ref):
    re, im = forward(real, imag, maps, count, tables)
    spec_ref[0], spec_ref[1] = re, im
    wide = jnp.concatenate([wt] * count, axis=1)
    part_ref[0], part_ref[1] = adjoint(re * wide, im * wide, maps, count, tables)


def block_row(turn, flip, extent):
    return pl.multiple_of(lax.bitwise_xor(jnp.int32(turn), flip) * extent, extent)


def at_home(kernel):
    def guarded(*refs):
        @pl.when(refs[0][1] == 1)
        def _():
            kernel(*refs)

    return guarded


def first_kernel(blocks, planes, info, steep_ref, *refs):
    messages, refs = refs[:blocks], refs[blocks:]
    tables, refs = refs[:10], refs[10:]
    maps, image, wt_ref, spec_ref, part_ref, odds, sems = refs
    extent = messages[0].shape[1]
    copies = []
    for k, msg in enumerate(messages):
        rows = pl.ds(block_row(k, info[0], extent), extent)
        copies += [
            pltpu.make_async_copy(msg.at[:planes], maps.at[:, rows], sems.at[0, k]),
            pltpu.make_async_copy(msg.at[pl.ds(planes, 2)], image.at[:, rows], sems.at[1, k]),
            pltpu.make_async_copy(msg.at[planes + 2], odds.at[rows], sems.at[2, k]),
        ]
    for copy in copies:
        copy.start()
    for copy in copies:
        copy.wait()
    wt = jax.nn.sigmoid(steep_ref[0] * odds[...]).T
    wt_ref[...] = wt
    normal(image[0], image[1], maps, planes // 2, tables, wt, spec_ref, part_ref)


def second_kernel(info, image, part, other, maps, wt_ref, *refs):
    tables, refs = refs[:10], refs[10:]
    residual_ref, dir_ref, sc_ref, spec_ref, part_ref = refs
    u = (image[0], image[1])
    q = tuple(part[i] + other[i] + DAMPING * u[i] for i in range(2))
    norm = inner(u, u)
    alpha = norm / inner(u, q)
    r = tuple(u[i] - alpha * q[i] for i in range(2))
    norm_next = inner(r, r)
    p = tuple(r[i] + (norm_next / norm) * u[i] for i in range(2))
    for i in range(2):
        residual_ref[i] = r[i]
        dir_ref[i] = p[i]
    sc_ref[0] = jnp.broadcast_to(alpha, sc_ref.shape[1:])
    sc_ref[1] = jnp.broadcast_to(norm_next, sc_ref.shape[1:])
    normal(p[0], p[1], maps, maps.shape[0] // 2, tables, wt_ref[...], spec_ref, part_ref)


def third_kernel(blocks, planes, info, image, res_ref, dir_ref, sc_in, part, other, maps,
                 wt_ref, spec0_ref, spec1_ref, *refs):
    messages, refs = refs[:blocks], refs[blocks:]
    tables, refs = refs[:10], refs[10:]
    sol_ref, p_ref, sc_ref, out_ref, data, recon, spec0, spec1, sems = refs
    extent = messages[0].shape[1]
    copies = []
    for k, msg in enumerate(messages):
        rows = pl.ds(block_row(k, info[0], extent), extent)
        copies += [
            pltpu.make_async_copy(msg.at[pl.ds(planes, 2)], recon.at[:, rows], sems.at[1, k]),
            pltpu.make_async_copy(msg.at[:planes], data.at[:, rows], sems.at[0, k]),
        ]
    copies += [
        pltpu.make_async_copy(spec0_ref, spec0, sems.at[2, 0]),
        pltpu.make_async_copy(spec1_ref, spec1, sems.at[2, 1]),
    ]
    for copy in copies:
        copy.start()
    count = planes // 2
    n = image.shape[1]
    alpha0, norm = sc_in[0, :1, :1], sc_in[1, :1, :1]
    p = (dir_ref[0], dir_ref[1])
    q = tuple(part[i] + other[i] + DAMPING * p[i] for i in range(2))
    alpha1 = norm / inner(p, q)
    r = tuple(res_ref[i] - alpha1 * q[i] for i in range(2))
    norm_next = inner(r, r)
    for i in range(2):
        sol_ref[i] = alpha0 * image[i] + alpha1 * p[i]
    p = tuple(r[i] + (norm_next / norm) * p[i] for i in range(2))
    p_ref[0], p_ref[1] = p
    re, im = forward(p[0], p[1], maps, count, tables)
    wide = jnp.concatenate([wt_ref[...]] * count, axis=1)
    energy = total(wide * (re * re + im * im))
    sc_ref[0] = jnp.broadcast_to(norm_next, sc_ref.shape[1:])
    sc_ref[1] = jnp.broadcast_to(inner(p, p), sc_ref.shape[1:])
    for copy in copies:
        copy.wait()
    est_re, est_im = forward(recon[0], recon[1], maps, count, tables)
    known = last = 0.0
    for c in range(count):
        s = slice(c * n, (c + 1) * n)
        diff_re = data[2 * c].T - est_re[:, s]
        diff_im = data[2 * c + 1].T - est_im[:, s]
        sol_re = alpha0 * spec0[0, :, s] + alpha1 * spec1[0, :, s]
        sol_im = alpha0 * spec0[1, :, s] + alpha1 * spec1[1, :, s]
        known = known + (sol_re * diff_re + sol_im * diff_im)
        last = last + (re[:, s] * diff_re + im[:, s] * diff_im)
    out_ref[:n] = known
    out_ref[n : 2 * n] = last
    out_ref[2 * n :] = jnp.broadcast_to(energy, (out_ref.shape[0] - 2 * n, n))


def fourth_kernel(info, mine, other, sol, p_ref, sc, *refs):
    outs, terms = refs[:-1], refs[-1]
    half = info[2]
    n = sol.shape[1]
    extent = outs[0].shape[1]
    energy = mine[2 * n :, :][:1, :1] + other[2 * n :, :][:1, :1] + DAMPING * sc[1, :1, :1]
    alpha = sc[0, :1, :1] / energy
    terms[...] = (
        (mine[:n] + other[:n]) + alpha * (mine[n : 2 * n] + other[n : 2 * n])
    ).T
    for k, out in enumerate(outs):
        rows = pl.ds(pl.multiple_of((half * len(outs) + k) * extent, extent), extent)
        out[0] = sol[0, rows] + alpha * p_ref[0, rows]
        out[1] = sol[1, rows] + alpha * p_ref[1, rows]
        out[2] = terms[rows]


def call(*args, **kwargs):
    def run(*operands):
        return pl.pallas_call(*args, compiler_params=PARAMS, **kwargs)(*operands)

    return run


VMEM = pl.BlockSpec(memory_space=pltpu.VMEM)
SMEM = pl.BlockSpec(memory_space=pltpu.SMEM)
ANY = pl.BlockSpec(memory_space=pl.ANY)
PARAMS = pltpu.CompilerParams(vmem_limit_bytes=48 << 20)


def shape(*dims):
    return jax.ShapeDtypeStruct(dims, F32)


def home_row(piece, blocks):
    first = blocks // 4
    return first if piece % 2 == 0 else blocks - 1 - first


def gather_pairs(turn, pieces, blocks):
    pairs = []
    for piece in range(pieces):
        for half in range(2):
            block = turn ^ half ^ (blocks // 2 if piece % 2 else 0)
            target = (piece - piece % 2 + half) * blocks + home_row(piece, blocks)
            pairs.append((piece * blocks + block, target))
    return pairs


def scatter_pairs(turn, pieces, blocks):
    pairs = []
    for piece in range(pieces):
        for half in range(2):
            source = (piece - piece % 2 + half) * blocks + home_row(piece, blocks)
            target = piece * blocks + turn + half * (blocks // 2)
            pairs.append((source, target))
    return pairs


def steps(
    upstream_loss_derivative,
    estimated_slice_image,
    receiver_profile_maps,
    measured_fourier_data,
    acquisition_choice_odds,
    sigmoid_steepness,
):
    blocks = lax.axis_size("rows")
    pieces = lax.axis_size("cuts")
    row = lax.axis_index("rows")
    half = lax.rem(lax.axis_index("cuts"), 2)
    upper = row >= blocks // 2
    home = (row == home_row(0, blocks)) | (row == home_row(1, blocks))
    flip = jnp.bitwise_xor(half, jnp.where(upper, blocks // 2, 0))
    info = jnp.stack([flip, home.astype(jnp.int32), half]).astype(jnp.int32)
    odd = lax.rem(row, 2)
    extent = upstream_loss_derivative.shape[3]
    n = upstream_loss_derivative.shape[4]
    coils = receiver_profile_maps.shape[1]
    planes = coils
    count = coils // 2
    tables = [jnp.asarray(t) for t in dft_tables(n)]
    swap = [(i, i ^ 1) for i in range(pieces)]

    maps = receiver_profile_maps.reshape(2, planes, extent, n)
    data = measured_fourier_data.reshape(2, planes, extent, n)
    upstream = upstream_loss_derivative.reshape(2, extent, n)
    recon = estimated_slice_image.reshape(2, extent, n)
    take = lambda values, i: lax.dynamic_index_in_dim(values, i, 0, keepdims=False)

    def build(values, *more):
        return [
            jnp.concatenate([take(values, i), *more], axis=0) for i in (odd, 1 - odd)
        ]

    def gather(sends, turns):
        return [lax.ppermute(sends[k % 2], BOTH, gather_pairs(k, pieces, blocks)) for k in turns]

    near, far = range(blocks // 2), range(blocks // 2, blocks)
    sends = build(maps, upstream, acquisition_choice_odds)
    first = gather(sends, near) + gather(sends, far)
    sends = build(data, recon)
    sends = lax.optimization_barrier((*sends, *first[: blocks // 2]))[:2]
    second = gather(sends, near)

    image, spectrum = shape(2, n, n), shape(2, n, count * n)
    scalars = shape(2, 8, 128)
    stacked = shape(planes, n, n)
    maps_full, u, wt, spec0, part0 = call(
        at_home(functools.partial(first_kernel, blocks, planes)),
        in_specs=[SMEM, SMEM] + [ANY] * blocks + [VMEM] * 10,
        out_specs=[VMEM] * 5,
        out_shape=[stacked, image, shape(n, n), spectrum, image],
        scratch_shapes=[pltpu.VMEM((n, n), F32), pltpu.SemaphoreType.DMA((3, blocks))],
    )(info, sigmoid_steepness, *first, *tables)
    other0 = lax.ppermute(part0, "cuts", swap)
    sends = lax.optimization_barrier((*sends, part0))[:2]
    second += gather(sends, far)
    res1, dir1, sc1, spec1, part1 = call(
        at_home(second_kernel),
        in_specs=[SMEM] + [VMEM] * 15,
        out_specs=[VMEM] * 5,
        out_shape=[image, image, scalars, spectrum, image],
    )(info, u, part0, other0, maps_full, wt, *tables)
    other1 = lax.ppermute(part1, "cuts", swap)
    sol2, dir2, sc2, mine = call(
        at_home(functools.partial(third_kernel, blocks, planes)),
        in_specs=[SMEM] + [VMEM] * 8 + [ANY] * 2 + [ANY] * blocks + [VMEM] * 10,
        out_specs=[VMEM] * 4,
        out_shape=[image, image, scalars, shape(2 * n + 8, n)],
        scratch_shapes=[
            pltpu.VMEM((planes, n, n), F32),
            pltpu.VMEM((2, n, n), F32),
            pltpu.VMEM((2, n, count * n), F32),
            pltpu.VMEM((2, n, count * n), F32),
            pltpu.SemaphoreType.DMA((3, blocks)),
        ],
    )(info, u, res1, dir1, sc1, part1, other1, maps_full, wt, spec0, spec1, *second, *tables)
    other = lax.ppermute(mine, "cuts", swap)
    turns = blocks // 2
    outs = call(
        at_home(fourth_kernel),
        in_specs=[SMEM] + [VMEM] * 5,
        out_specs=[VMEM] * turns,
        out_shape=[shape(3, extent, n)] * turns,
        scratch_shapes=[pltpu.VMEM((n, n), F32)],
    )(info, mine, other, sol2, dir2, sc2)
    parts = [
        lax.ppermute(outs[k], BOTH, scatter_pairs(k, pieces, blocks)) for k in range(turns)
    ]
    whole = parts[0]
    for part in parts[1:]:
        whole = whole + part
    term = whole[2]
    step = 1
    while step < pieces:
        term = term + lax.ppermute(term, "cuts", [(i, i ^ step) for i in range(pieces)])
        step *= 2
    steep = sigmoid_steepness[0]
    weights = jax.nn.sigmoid(steep * acquisition_choice_odds)
    slices = upstream_loss_derivative.shape[0] * pieces
    gradient = steep * weights * (1.0 - weights) * term[None] / slices
    return whole[:2].reshape(upstream_loss_derivative.shape), gradient


def solution(mesh):
    return jax.shard_map(
        steps,
        mesh=mesh,
        in_specs=(
            P("cuts", None, None, "rows", None),
            P("cuts", None, None, "rows", None),
            P("cuts", None, None, "rows", None),
            P("cuts", None, None, None, "rows", None),
            P(None, "rows", None),
            P(),
        ),
        out_specs=(P("cuts", None, None, "rows", None), P(None, "rows", None)),
        check_vma=False,
    )
```

```python
import functools
import math

import jax
import jax.numpy as jnp
import ml_dtypes
import numpy as np
from jax import lax
from jax.experimental import pallas as pl
from jax.experimental.pallas import tpu as pltpu
from jax.sharding import PartitionSpec as P


DAMPING = 0.1
F32 = jnp.float32
BF16 = jnp.bfloat16
BOTH = ("cuts", "rows")


def host_split(table):
    high = table.astype(np.float32).astype(ml_dtypes.bfloat16)
    low = (table - high.astype(np.float64)).astype(ml_dtypes.bfloat16)
    return high, low


def dft_tables(extent):
    position = np.arange(extent)
    angle = (np.outer(position, position) % extent) * (2.0 * math.pi / extent)
    cos = np.cos(angle) / math.sqrt(extent)
    sin = np.sin(angle) / math.sqrt(extent)
    out = [*host_split(cos)]
    for imag in (-sin, sin):
        out += [*host_split(imag - cos), *host_split(cos + imag)]
    return out


def split(values):
    high = values.astype(BF16)
    low = (values - high.astype(F32)).astype(BF16)
    return high, low


def dot(first, second):
    return lax.dot_general(
        first, second, (((1,), (0,)), ((), ())), preferred_element_type=F32
    )


def by_right(values, high, low):
    vh, vl = split(values)
    return dot(vh, high) + dot(vl, high) + dot(vh, low)


def by_left(values, high, low):
    vh, vl = split(values)
    return dot(high, vh) + dot(high, vl) + dot(low, vh)


def complex_product(multiply, real, imag, t):
    shared = multiply(real + imag, t[0][...], t[1][...])
    cross_real = multiply(real, t[2][...], t[3][...])
    cross_imag = multiply(imag, t[4][...], t[5][...])
    return shared - cross_imag, shared + cross_real


def pick(tables, inverse):
    return [*tables[:2], *(tables[6:10] if inverse else tables[2:6])]


def to_lanes(values, count):
    rows = values.shape[0] // count
    return jnp.concatenate([values[c * rows : (c + 1) * rows] for c in range(count)], axis=1)


def to_rows(values, count):
    cols = values.shape[1] // count
    return jnp.concatenate([values[:, c * cols : (c + 1) * cols] for c in range(count)], axis=0)


def forward(real, imag, maps, count, tables):
    t = pick(tables, False)
    prod_real = jnp.concatenate(
        [maps[2 * c] * real - maps[2 * c + 1] * imag for c in range(count)], axis=0
    )
    prod_imag = jnp.concatenate(
        [maps[2 * c] * imag + maps[2 * c + 1] * real for c in range(count)], axis=0
    )
    re, im = complex_product(by_right, prod_real, prod_imag, t)
    return complex_product(by_left, to_lanes(re, count), to_lanes(im, count), t)


def adjoint(re, im, maps, count, tables):
    t = pick(tables, True)
    re, im = complex_product(by_left, re, im, t)
    re, im = complex_product(by_right, to_rows(re, count), to_rows(im, count), t)
    rows = re.shape[0] // count
    out_real = out_imag = 0.0
    for c in range(count):
        a, b = re[c * rows : (c + 1) * rows], im[c * rows : (c + 1) * rows]
        sr, si = maps[2 * c], maps[2 * c + 1]
        out_real = out_real + (sr * a + si * b)
        out_imag = out_imag + (sr * b - si * a)
    return out_real, out_imag


def total(values):
    return jnp.sum(jnp.sum(values, axis=0, keepdims=True), axis=1, keepdims=True)


def inner(first, second):
    return total(first[0] * second[0] + first[1] * second[1])


def normal(real, imag, maps, count, tables, wt, spec_ref, part_ref):
    re, im = forward(real, imag, maps, count, tables)
    spec_ref[0], spec_ref[1] = re, im
    wide = jnp.concatenate([wt] * count, axis=1)
    part_ref[0], part_ref[1] = adjoint(re * wide, im * wide, maps, count, tables)


def block_of(turn, half, column, blocks):
    return ((turn % (blocks // 2)) ^ half) * 2 + (column ^ (2 * turn // blocks))


def block_row(turn, info, blocks, extent):
    across = lax.bitwise_xor(jnp.int32(turn % (blocks // 2)), info[2])
    block = across * 2 + lax.bitwise_xor(info[0], jnp.int32(2 * turn // blocks))
    return pl.multiple_of(block * extent, extent)


def at_home(kernel):
    def guarded(*refs):
        @pl.when(refs[0][1] == 1)
        def _():
            kernel(*refs)

    return guarded


def first_kernel(blocks, planes, info, steep_ref, *refs):
    messages, refs = refs[:blocks], refs[blocks:]
    tables, refs = refs[:10], refs[10:]
    maps, image, wt_ref, spec_ref, part_ref, odds, sems = refs
    extent = messages[0].shape[1]
    copies = []
    for k, msg in enumerate(messages):
        rows = pl.ds(block_row(k, info, blocks, extent), extent)
        copies += [
            pltpu.make_async_copy(msg.at[:planes], maps.at[:, rows], sems.at[0, k]),
            pltpu.make_async_copy(msg.at[pl.ds(planes, 2)], image.at[:, rows], sems.at[1, k]),
            pltpu.make_async_copy(msg.at[planes + 2], odds.at[rows], sems.at[2, k]),
        ]
    for copy in copies:
        copy.start()
    for copy in copies:
        copy.wait()
    wt = jax.nn.sigmoid(steep_ref[0] * odds[...]).T
    wt_ref[...] = wt
    normal(image[0], image[1], maps, planes // 2, tables, wt, spec_ref, part_ref)


def second_kernel(info, image, part, other, maps, wt_ref, *refs):
    tables, refs = refs[:10], refs[10:]
    residual_ref, dir_ref, sc_ref, spec_ref, part_ref = refs
    u = (image[0], image[1])
    q = tuple(part[i] + other[i] + DAMPING * u[i] for i in range(2))
    norm = inner(u, u)
    alpha = norm / inner(u, q)
    r = tuple(u[i] - alpha * q[i] for i in range(2))
    norm_next = inner(r, r)
    p = tuple(r[i] + (norm_next / norm) * u[i] for i in range(2))
    for i in range(2):
        residual_ref[i] = r[i]
        dir_ref[i] = p[i]
    sc_ref[0] = jnp.broadcast_to(alpha, sc_ref.shape[1:])
    sc_ref[1] = jnp.broadcast_to(norm_next, sc_ref.shape[1:])
    normal(p[0], p[1], maps, maps.shape[0] // 2, tables, wt_ref[...], spec_ref, part_ref)


def third_kernel(blocks, planes, info, image, res_ref, dir_ref, sc_in, part, other, maps,
                 wt_ref, spec0_ref, spec1_ref, *refs):
    messages, refs = refs[:blocks], refs[blocks:]
    tables, refs = refs[:10], refs[10:]
    sol_ref, p_ref, sc_ref, out_ref, data, recon, spec0, spec1, sems = refs
    extent = messages[0].shape[1]
    copies = []
    for k, msg in enumerate(messages):
        rows = pl.ds(block_row(k, info, blocks, extent), extent)
        copies += [
            pltpu.make_async_copy(msg.at[pl.ds(planes, 2)], recon.at[:, rows], sems.at[1, k]),
            pltpu.make_async_copy(msg.at[:planes], data.at[:, rows], sems.at[0, k]),
        ]
    copies += [
        pltpu.make_async_copy(spec0_ref, spec0, sems.at[2, 0]),
        pltpu.make_async_copy(spec1_ref, spec1, sems.at[2, 1]),
    ]
    for copy in copies:
        copy.start()
    count = planes // 2
    n = image.shape[1]
    alpha0, norm = sc_in[0, :1, :1], sc_in[1, :1, :1]
    p = (dir_ref[0], dir_ref[1])
    q = tuple(part[i] + other[i] + DAMPING * p[i] for i in range(2))
    alpha1 = norm / inner(p, q)
    r = tuple(res_ref[i] - alpha1 * q[i] for i in range(2))
    norm_next = inner(r, r)
    for i in range(2):
        sol_ref[i] = alpha0 * image[i] + alpha1 * p[i]
    p = tuple(r[i] + (norm_next / norm) * p[i] for i in range(2))
    p_ref[0], p_ref[1] = p
    re, im = forward(p[0], p[1], maps, count, tables)
    wide = jnp.concatenate([wt_ref[...]] * count, axis=1)
    energy = total(wide * (re * re + im * im))
    sc_ref[0] = jnp.broadcast_to(norm_next, sc_ref.shape[1:])
    sc_ref[1] = jnp.broadcast_to(inner(p, p), sc_ref.shape[1:])
    for copy in copies:
        copy.wait()
    est_re, est_im = forward(recon[0], recon[1], maps, count, tables)
    known = last = 0.0
    for c in range(count):
        s = slice(c * n, (c + 1) * n)
        diff_re = data[2 * c].T - est_re[:, s]
        diff_im = data[2 * c + 1].T - est_im[:, s]
        sol_re = alpha0 * spec0[0, :, s] + alpha1 * spec1[0, :, s]
        sol_im = alpha0 * spec0[1, :, s] + alpha1 * spec1[1, :, s]
        known = known + (sol_re * diff_re + sol_im * diff_im)
        last = last + (re[:, s] * diff_re + im[:, s] * diff_im)
    out_ref[:n] = known
    out_ref[n : 2 * n] = last
    out_ref[2 * n :] = jnp.broadcast_to(energy, (out_ref.shape[0] - 2 * n, n))


def fourth_kernel(info, mine, other, sol, p_ref, sc, *refs):
    outs, terms = refs[:-1], refs[-1]
    half = info[2]
    n = sol.shape[1]
    extent = outs[0].shape[1]
    energy = mine[2 * n :, :][:1, :1] + other[2 * n :, :][:1, :1] + DAMPING * sc[1, :1, :1]
    alpha = sc[0, :1, :1] / energy
    terms[...] = (
        (mine[:n] + other[:n]) + alpha * (mine[n : 2 * n] + other[n : 2 * n])
    ).T
    for k, out in enumerate(outs):
        rows = pl.ds(pl.multiple_of((half * len(outs) + k) * extent, extent), extent)
        out[0] = sol[0, rows] + alpha * p_ref[0, rows]
        out[1] = sol[1, rows] + alpha * p_ref[1, rows]
        out[2] = terms[rows]


def call(*args, **kwargs):
    def run(*operands):
        return pl.pallas_call(*args, compiler_params=PARAMS, **kwargs)(*operands)

    return run


VMEM = pl.BlockSpec(memory_space=pltpu.VMEM)
SMEM = pl.BlockSpec(memory_space=pltpu.SMEM)
ANY = pl.BlockSpec(memory_space=pl.ANY)
PARAMS = pltpu.CompilerParams(vmem_limit_bytes=24 << 20)


def shape(*dims):
    return jax.ShapeDtypeStruct(dims, F32)


def home_row(piece, blocks):
    first = blocks // 4
    return first if piece % 2 == 0 else blocks - 1 - first


def gather_pairs(turn, pieces, blocks):
    pairs = []
    for piece in range(pieces):
        for half in range(2):
            block = block_of(turn, half, piece % 2, blocks)
            target = (piece - piece % 2 + half) * blocks + home_row(piece, blocks)
            pairs.append((piece * blocks + block, target))
    return pairs


def scatter_pairs(turn, pieces, blocks):
    pairs = []
    for piece in range(pieces):
        for half in range(2):
            source = (piece - piece % 2 + half) * blocks + home_row(piece, blocks)
            target = piece * blocks + turn + half * (blocks // 2)
            pairs.append((source, target))
    return pairs


def steps(
    upstream_loss_derivative,
    estimated_slice_image,
    receiver_profile_maps,
    measured_fourier_data,
    acquisition_choice_odds,
    sigmoid_steepness,
):
    blocks = lax.axis_size("rows")
    pieces = lax.axis_size("cuts")
    row = lax.axis_index("rows")
    half = lax.rem(lax.axis_index("cuts"), 2)
    column = (row == home_row(1, blocks)).astype(jnp.int32)
    home = column + (row == home_row(0, blocks)).astype(jnp.int32)
    info = jnp.stack([column, home, half]).astype(jnp.int32)
    odd = lax.rem(row // 2, 2)
    extent = upstream_loss_derivative.shape[3]
    n = upstream_loss_derivative.shape[4]
    coils = receiver_profile_maps.shape[1]
    planes = coils
    count = coils // 2
    tables = [jnp.asarray(t) for t in dft_tables(n)]
    swap = [(i, i ^ 1) for i in range(pieces)]

    maps = receiver_profile_maps.reshape(2, planes, extent, n)
    data = measured_fourier_data.reshape(2, planes, extent, n)
    upstream = upstream_loss_derivative.reshape(2, extent, n)
    recon = estimated_slice_image.reshape(2, extent, n)
    take = lambda values, i: lax.dynamic_index_in_dim(values, i, 0, keepdims=False)

    def build(values, *more):
        return [
            jnp.concatenate([take(values, i), *more], axis=0) for i in (odd, 1 - odd)
        ]

    def gather(sends, turns):
        return [lax.ppermute(sends[k % 2], BOTH, gather_pairs(k, pieces, blocks)) for k in turns]

    near, far = range(blocks // 2), range(blocks // 2, blocks)
    sends = build(maps, upstream, acquisition_choice_odds)
    first = gather(sends, near) + gather(sends, far)
    sends = build(data, recon)
    second = gather(sends, near) + gather(sends, far)

    image, spectrum = shape(2, n, n), shape(2, n, count * n)
    scalars = shape(2, 8, 128)
    stacked = shape(planes, n, n)
    maps_full, u, wt, spec0, part0 = call(
        at_home(functools.partial(first_kernel, blocks, planes)),
        in_specs=[SMEM, SMEM] + [ANY] * blocks + [VMEM] * 10,
        out_specs=[VMEM] * 5,
        out_shape=[stacked, image, shape(n, n), spectrum, image],
        scratch_shapes=[pltpu.VMEM((n, n), F32), pltpu.SemaphoreType.DMA((3, blocks))],
    )(info, sigmoid_steepness, *first, *tables)
    other0 = lax.ppermute(part0, "cuts", swap)
    res1, dir1, sc1, spec1, part1 = call(
        at_home(second_kernel),
        in_specs=[SMEM] + [VMEM] * 15,
        out_specs=[VMEM] * 5,
        out_shape=[image, image, scalars, spectrum, image],
    )(info, u, part0, other0, maps_full, wt, *tables)
    other1 = lax.ppermute(part1, "cuts", swap)
    sol2, dir2, sc2, mine = call(
        at_home(functools.partial(third_kernel, blocks, planes)),
        in_specs=[SMEM] + [VMEM] * 8 + [ANY] * 2 + [ANY] * blocks + [VMEM] * 10,
        out_specs=[VMEM] * 4,
        out_shape=[image, image, scalars, shape(2 * n + 8, n)],
        scratch_shapes=[
            pltpu.VMEM((planes, n, n), F32),
            pltpu.VMEM((2, n, n), F32),
            pltpu.VMEM((2, n, count * n), F32),
            pltpu.VMEM((2, n, count * n), F32),
            pltpu.SemaphoreType.DMA((3, blocks)),
        ],
    )(info, u, res1, dir1, sc1, part1, other1, maps_full, wt, spec0, spec1, *second, *tables)
    other = lax.ppermute(mine, "cuts", swap)
    turns = blocks // 2
    outs = call(
        at_home(fourth_kernel),
        in_specs=[SMEM] + [VMEM] * 5,
        out_specs=[VMEM] * turns,
        out_shape=[shape(3, extent, n)] * turns,
        scratch_shapes=[pltpu.VMEM((n, n), F32)],
    )(info, mine, other, sol2, dir2, sc2)
    parts = [
        lax.ppermute(outs[k], BOTH, scatter_pairs(k, pieces, blocks)) for k in range(turns)
    ]
    whole = parts[0]
    for part in parts[1:]:
        whole = whole + part
    term = whole[2]
    step = 1
    while step < pieces:
        term = term + lax.ppermute(term, "cuts", [(i, i ^ step) for i in range(pieces)])
        step *= 2
    steep = sigmoid_steepness[0]
    weights = jax.nn.sigmoid(steep * acquisition_choice_odds)
    slices = upstream_loss_derivative.shape[0] * pieces
    gradient = steep * weights * (1.0 - weights) * term[None] / slices
    return whole[:2].reshape(upstream_loss_derivative.shape), gradient


def solution(mesh):
    return jax.shard_map(
        steps,
        mesh=mesh,
        in_specs=(
            P("cuts", None, None, "rows", None),
            P("cuts", None, None, "rows", None),
            P("cuts", None, None, "rows", None),
            P("cuts", None, None, None, "rows", None),
            P(None, "rows", None),
            P(),
        ),
        out_specs=(P("cuts", None, None, "rows", None), P(None, "rows", None)),
        check_vma=False,
    )
```

```python
import functools
import math

import jax
import jax.numpy as jnp
import ml_dtypes
import numpy as np
from jax import lax
from jax.experimental import pallas as pl
from jax.experimental.pallas import tpu as pltpu
from jax.sharding import PartitionSpec as P


DAMPING = 0.1
F32 = jnp.float32
BF16 = jnp.bfloat16
BOTH = ("cuts", "rows")


def host_split(table):
    high = table.astype(np.float32).astype(ml_dtypes.bfloat16)
    low = (table - high.astype(np.float64)).astype(ml_dtypes.bfloat16)
    return high, low


def dft_tables(extent):
    position = np.arange(extent)
    angle = (np.outer(position, position) % extent) * (2.0 * math.pi / extent)
    cos = np.cos(angle) / math.sqrt(extent)
    sin = np.sin(angle) / math.sqrt(extent)
    out = [*host_split(cos)]
    for imag in (-sin, sin):
        out += [*host_split(imag - cos), *host_split(cos + imag)]
    return out


def split(values):
    high = values.astype(BF16)
    low = (values - high.astype(F32)).astype(BF16)
    return high, low


def dot(first, second):
    return lax.dot_general(
        first, second, (((1,), (0,)), ((), ())), preferred_element_type=F32
    )


def by_right(values, high, low):
    vh, vl = split(values)
    return dot(vh, high) + dot(vl, high) + dot(vh, low)


def by_left(values, high, low):
    vh, vl = split(values)
    return dot(high, vh) + dot(high, vl) + dot(low, vh)


def complex_product(multiply, real, imag, t):
    shared = multiply(real + imag, t[0][...], t[1][...])
    cross_real = multiply(real, t[2][...], t[3][...])
    cross_imag = multiply(imag, t[4][...], t[5][...])
    return shared - cross_imag, shared + cross_real


def pick(tables, inverse):
    return [*tables[:2], *(tables[6:10] if inverse else tables[2:6])]


def to_lanes(values, count):
    rows = values.shape[0] // count
    return jnp.concatenate([values[c * rows : (c + 1) * rows] for c in range(count)], axis=1)


def to_rows(values, count):
    cols = values.shape[1] // count
    return jnp.concatenate([values[:, c * cols : (c + 1) * cols] for c in range(count)], axis=0)


def forward(real, imag, maps, count, tables):
    t = pick(tables, False)
    prod_real = jnp.concatenate(
        [maps[2 * c] * real - maps[2 * c + 1] * imag for c in range(count)], axis=0
    )
    prod_imag = jnp.concatenate(
        [maps[2 * c] * imag + maps[2 * c + 1] * real for c in range(count)], axis=0
    )
    re, im = complex_product(by_right, prod_real, prod_imag, t)
    return complex_product(by_left, to_lanes(re, count), to_lanes(im, count), t)


def adjoint(re, im, maps, count, tables):
    t = pick(tables, True)
    re, im = complex_product(by_left, re, im, t)
    re, im = complex_product(by_right, to_rows(re, count), to_rows(im, count), t)
    rows = re.shape[0] // count
    out_real = out_imag = 0.0
    for c in range(count):
        a, b = re[c * rows : (c + 1) * rows], im[c * rows : (c + 1) * rows]
        sr, si = maps[2 * c], maps[2 * c + 1]
        out_real = out_real + (sr * a + si * b)
        out_imag = out_imag + (sr * b - si * a)
    return out_real, out_imag


def total(values):
    return jnp.sum(jnp.sum(values, axis=0, keepdims=True), axis=1, keepdims=True)


def inner(first, second):
    return total(first[0] * second[0] + first[1] * second[1])


def normal(real, imag, maps, count, tables, wt, spec_ref, part_ref):
    re, im = forward(real, imag, maps, count, tables)
    spec_ref[0], spec_ref[1] = re, im
    wide = jnp.concatenate([wt] * count, axis=1)
    part_ref[0], part_ref[1] = adjoint(re * wide, im * wide, maps, count, tables)


def block_of(turn, half, column, blocks):
    if turn < blocks // 2:
        return turn ^ half, column
    return (turn - blocks // 2) ^ half ^ (2 - 2 * column), 1 - column


def block_row(turn, info, blocks, extent):
    column, half = info[0], info[2]
    pair = lax.bitwise_xor(jnp.int32(turn % (blocks // 2)), half)
    if turn >= blocks // 2:
        pair = lax.bitwise_xor(pair, 2 - 2 * column)
        column = 1 - column
    return pl.multiple_of((pair * 2 + column) * extent, extent)


def at_home(kernel):
    def guarded(*refs):
        @pl.when(refs[0][1] == 1)
        def _():
            kernel(*refs)

    return guarded


def first_kernel(blocks, planes, info, steep_ref, *refs):
    messages, refs = refs[:blocks], refs[blocks:]
    tables, refs = refs[:10], refs[10:]
    maps, image, wt_ref, spec_ref, part_ref, odds, sems = refs
    extent = messages[0].shape[1]
    copies = []
    for k, msg in enumerate(messages):
        rows = pl.ds(block_row(k, info, blocks, extent), extent)
        copies += [
            pltpu.make_async_copy(msg.at[:planes], maps.at[:, rows], sems.at[0, k]),
            pltpu.make_async_copy(msg.at[pl.ds(planes, 2)], image.at[:, rows], sems.at[1, k]),
            pltpu.make_async_copy(msg.at[planes + 2], odds.at[rows], sems.at[2, k]),
        ]
    for copy in copies:
        copy.start()
    for copy in copies:
        copy.wait()
    wt = jax.nn.sigmoid(steep_ref[0] * odds[...]).T
    wt_ref[...] = wt
    normal(image[0], image[1], maps, planes // 2, tables, wt, spec_ref, part_ref)


def second_kernel(info, image, part, other, maps, wt_ref, *refs):
    tables, refs = refs[:10], refs[10:]
    residual_ref, dir_ref, sc_ref, spec_ref, part_ref = refs
    u = (image[0], image[1])
    q = tuple(part[i] + other[i] + DAMPING * u[i] for i in range(2))
    norm = inner(u, u)
    alpha = norm / inner(u, q)
    r = tuple(u[i] - alpha * q[i] for i in range(2))
    norm_next = inner(r, r)
    p = tuple(r[i] + (norm_next / norm) * u[i] for i in range(2))
    for i in range(2):
        residual_ref[i] = r[i]
        dir_ref[i] = p[i]
    sc_ref[0] = jnp.broadcast_to(alpha, sc_ref.shape[1:])
    sc_ref[1] = jnp.broadcast_to(norm_next, sc_ref.shape[1:])
    normal(p[0], p[1], maps, maps.shape[0] // 2, tables, wt_ref[...], spec_ref, part_ref)


def third_kernel(blocks, planes, info, image, res_ref, dir_ref, sc_in, part, other, maps,
                 wt_ref, spec0_ref, spec1_ref, *refs):
    messages, refs = refs[:blocks], refs[blocks:]
    tables, refs = refs[:10], refs[10:]
    sol_ref, p_ref, sc_ref, out_ref, data, recon, spec0, spec1, sems = refs
    extent = messages[0].shape[1]
    copies = []
    for k, msg in enumerate(messages):
        rows = pl.ds(block_row(k, info, blocks, extent), extent)
        copies += [
            pltpu.make_async_copy(msg.at[pl.ds(planes, 2)], recon.at[:, rows], sems.at[1, k]),
            pltpu.make_async_copy(msg.at[:planes], data.at[:, rows], sems.at[0, k]),
        ]
    copies += [
        pltpu.make_async_copy(spec0_ref, spec0, sems.at[2, 0]),
        pltpu.make_async_copy(spec1_ref, spec1, sems.at[2, 1]),
    ]
    for copy in copies:
        copy.start()
    count = planes // 2
    n = image.shape[1]
    alpha0, norm = sc_in[0, :1, :1], sc_in[1, :1, :1]
    p = (dir_ref[0], dir_ref[1])
    q = tuple(part[i] + other[i] + DAMPING * p[i] for i in range(2))
    alpha1 = norm / inner(p, q)
    r = tuple(res_ref[i] - alpha1 * q[i] for i in range(2))
    norm_next = inner(r, r)
    for i in range(2):
        sol_ref[i] = alpha0 * image[i] + alpha1 * p[i]
    p = tuple(r[i] + (norm_next / norm) * p[i] for i in range(2))
    p_ref[0], p_ref[1] = p
    re, im = forward(p[0], p[1], maps, count, tables)
    wide = jnp.concatenate([wt_ref[...]] * count, axis=1)
    energy = total(wide * (re * re + im * im))
    sc_ref[0] = jnp.broadcast_to(norm_next, sc_ref.shape[1:])
    sc_ref[1] = jnp.broadcast_to(inner(p, p), sc_ref.shape[1:])
    for copy in copies:
        copy.wait()
    est_re, est_im = forward(recon[0], recon[1], maps, count, tables)
    known = last = 0.0
    for c in range(count):
        s = slice(c * n, (c + 1) * n)
        diff_re = data[2 * c].T - est_re[:, s]
        diff_im = data[2 * c + 1].T - est_im[:, s]
        sol_re = alpha0 * spec0[0, :, s] + alpha1 * spec1[0, :, s]
        sol_im = alpha0 * spec0[1, :, s] + alpha1 * spec1[1, :, s]
        known = known + (sol_re * diff_re + sol_im * diff_im)
        last = last + (re[:, s] * diff_re + im[:, s] * diff_im)
    out_ref[:n] = known
    out_ref[n : 2 * n] = last
    out_ref[2 * n :] = jnp.broadcast_to(energy, (out_ref.shape[0] - 2 * n, n))


def fourth_kernel(info, mine, other, sol, p_ref, sc, *refs):
    outs, terms = refs[:-1], refs[-1]
    half = info[2]
    n = sol.shape[1]
    extent = outs[0].shape[1]
    energy = mine[2 * n :, :][:1, :1] + other[2 * n :, :][:1, :1] + DAMPING * sc[1, :1, :1]
    alpha = sc[0, :1, :1] / energy
    terms[...] = (
        (mine[:n] + other[:n]) + alpha * (mine[n : 2 * n] + other[n : 2 * n])
    ).T
    for k, out in enumerate(outs):
        rows = pl.ds(pl.multiple_of((half * len(outs) + k) * extent, extent), extent)
        out[0] = sol[0, rows] + alpha * p_ref[0, rows]
        out[1] = sol[1, rows] + alpha * p_ref[1, rows]
        out[2] = terms[rows]


def call(*args, **kwargs):
    def run(*operands):
        return pl.pallas_call(*args, compiler_params=PARAMS, **kwargs)(*operands)

    return run


VMEM = pl.BlockSpec(memory_space=pltpu.VMEM)
SMEM = pl.BlockSpec(memory_space=pltpu.SMEM)
ANY = pl.BlockSpec(memory_space=pl.ANY)
PARAMS = pltpu.CompilerParams(vmem_limit_bytes=24 << 20)


def shape(*dims):
    return jax.ShapeDtypeStruct(dims, F32)


def home_row(piece, blocks):
    first = blocks // 4
    return first if piece % 2 == 0 else blocks - 1 - first


def detour(piece, blocks):
    return (blocks // 2 - 1) * (piece % 2)


def gather_pairs(turn, pieces, blocks, moved):
    pairs = []
    for piece in range(pieces):
        for half in range(2):
            pair, column = block_of(turn, half, piece % 2, blocks)
            source = piece * blocks + pair * 2 + column
            if column != piece % 2 and moved(piece, pair):
                source = (piece ^ 1) * blocks + pair * 2 + 1 - column
            target = (piece - piece % 2 + half) * blocks + home_row(piece, blocks)
            pairs.append((source, target))
    return pairs


def move_pairs(pieces, blocks, moved):
    pairs = []
    for piece in range(pieces):
        for pair in range(blocks // 2):
            if moved(piece, pair):
                column = piece % 2
                source = piece * blocks + pair * 2 + 1 - column
                pairs.append((source, (piece ^ 1) * blocks + pair * 2 + column))
    return pairs


def scatter_pairs(turn, pieces, blocks):
    pairs = []
    for piece in range(pieces):
        for half in range(2):
            source = (piece - piece % 2 + half) * blocks + home_row(piece, blocks)
            target = piece * blocks + turn + half * (blocks // 2)
            pairs.append((source, target))
    return pairs


def steps(
    upstream_loss_derivative,
    estimated_slice_image,
    receiver_profile_maps,
    measured_fourier_data,
    acquisition_choice_odds,
    sigmoid_steepness,
):
    blocks = lax.axis_size("rows")
    pieces = lax.axis_size("cuts")
    row = lax.axis_index("rows")
    half = lax.rem(lax.axis_index("cuts"), 2)
    column = (row == home_row(1, blocks)).astype(jnp.int32)
    home = column + (row == home_row(0, blocks)).astype(jnp.int32)
    info = jnp.stack([column, home, half]).astype(jnp.int32)
    odd = lax.rem(row // 2, 2)
    extent = upstream_loss_derivative.shape[3]
    n = upstream_loss_derivative.shape[4]
    coils = receiver_profile_maps.shape[1]
    planes = coils
    count = coils // 2
    tables = [jnp.asarray(t) for t in dft_tables(n)]
    swap = [(i, i ^ 1) for i in range(pieces)]

    maps = receiver_profile_maps.reshape(2, planes, extent, n)
    data = measured_fourier_data.reshape(2, planes, extent, n)
    upstream = upstream_loss_derivative.reshape(2, extent, n)
    recon = estimated_slice_image.reshape(2, extent, n)
    take = lambda values, i: lax.dynamic_index_in_dim(values, i, 0, keepdims=False)

    def build(values, *more):
        sends = [jnp.concatenate([take(values, i), *more], axis=0) for i in (odd, 1 - odd)]
        return lax.optimization_barrier(sends)

    away = lax.rem(row + half, 2) == 1
    far_end = row // 2 == (blocks // 2 - 1) * (1 - half)

    def ends(piece, pair):
        return pair == detour(piece, blocks)

    def every(piece, pair):
        return True

    def move(sends, moved):
        both = jnp.concatenate(sends, axis=0)
        return jnp.split(lax.ppermute(both, BOTH, move_pairs(pieces, blocks, moved)), 2)

    def gather(sends, turns, moved):
        return {
            k: lax.ppermute(sends[k % 2], BOTH, gather_pairs(k, pieces, blocks, moved))
            for k in turns
        }

    turns = blocks // 2
    near, far = range(turns), range(turns, blocks)
    late = sorted({turns + 2, turns + 3, blocks - 2, blocks - 1})
    sends = build(maps, upstream, acquisition_choice_odds)
    carried = move(sends, ends)
    first = gather(sends, near, ends)
    first |= gather(sends, [k for k in far if k not in late], ends)
    sends = [jnp.where(away & far_end, c, s) for c, s in zip(carried, sends)]
    first |= gather(sends, late, ends)
    first = [first[k] for k in range(blocks)]
    sends = build(data, recon)
    carried = move(sends, every)
    second = gather(sends, near, every)
    sends = [jnp.where(away, c, s) for c, s in zip(carried, sends)]
    second |= gather(sends, far, every)
    second = [second[k] for k in range(blocks)]

    image, spectrum = shape(2, n, n), shape(2, n, count * n)
    scalars = shape(2, 8, 128)
    stacked = shape(planes, n, n)
    maps_full, u, wt, spec0, part0 = call(
        at_home(functools.partial(first_kernel, blocks, planes)),
        in_specs=[SMEM, SMEM] + [ANY] * blocks + [VMEM] * 10,
        out_specs=[VMEM] * 5,
        out_shape=[stacked, image, shape(n, n), spectrum, image],
        scratch_shapes=[pltpu.VMEM((n, n), F32), pltpu.SemaphoreType.DMA((3, blocks))],
    )(info, sigmoid_steepness, *first, *tables)
    other0 = lax.ppermute(part0, "cuts", swap)
    res1, dir1, sc1, spec1, part1 = call(
        at_home(second_kernel),
        in_specs=[SMEM] + [VMEM] * 15,
        out_specs=[VMEM] * 5,
        out_shape=[image, image, scalars, spectrum, image],
    )(info, u, part0, other0, maps_full, wt, *tables)
    other1 = lax.ppermute(part1, "cuts", swap)
    sol2, dir2, sc2, mine = call(
        at_home(functools.partial(third_kernel, blocks, planes)),
        in_specs=[SMEM] + [VMEM] * 8 + [ANY] * 2 + [ANY] * blocks + [VMEM] * 10,
        out_specs=[VMEM] * 4,
        out_shape=[image, image, scalars, shape(2 * n + 8, n)],
        scratch_shapes=[
            pltpu.VMEM((planes, n, n), F32),
            pltpu.VMEM((2, n, n), F32),
            pltpu.VMEM((2, n, count * n), F32),
            pltpu.VMEM((2, n, count * n), F32),
            pltpu.SemaphoreType.DMA((3, blocks)),
        ],
    )(info, u, res1, dir1, sc1, part1, other1, maps_full, wt, spec0, spec1, *second, *tables)
    other = lax.ppermute(mine, "cuts", swap)
    outs = call(
        at_home(fourth_kernel),
        in_specs=[SMEM] + [VMEM] * 5,
        out_specs=[VMEM] * turns,
        out_shape=[shape(3, extent, n)] * turns,
        scratch_shapes=[pltpu.VMEM((n, n), F32)],
    )(info, mine, other, sol2, dir2, sc2)
    parts = [
        lax.ppermute(outs[k], BOTH, scatter_pairs(k, pieces, blocks)) for k in range(turns)
    ]
    whole = parts[0]
    for part in parts[1:]:
        whole = whole + part
    term = whole[2]
    step = 1
    while step < pieces:
        term = term + lax.ppermute(term, "cuts", [(i, i ^ step) for i in range(pieces)])
        step *= 2
    steep = sigmoid_steepness[0]
    weights = jax.nn.sigmoid(steep * acquisition_choice_odds)
    slices = upstream_loss_derivative.shape[0] * pieces
    gradient = steep * weights * (1.0 - weights) * term[None] / slices
    return whole[:2].reshape(upstream_loss_derivative.shape), gradient


def solution(mesh):
    return jax.shard_map(
        steps,
        mesh=mesh,
        in_specs=(
            P("cuts", None, None, "rows", None),
            P("cuts", None, None, "rows", None),
            P("cuts", None, None, "rows", None),
            P("cuts", None, None, None, "rows", None),
            P(None, "rows", None),
            P(),
        ),
        out_specs=(P("cuts", None, None, "rows", None), P(None, "rows", None)),
        check_vma=False,
    )
```

```python
import functools
import math

import jax
import jax.numpy as jnp
import ml_dtypes
import numpy as np
from jax import lax
from jax.experimental import pallas as pl
from jax.experimental.pallas import tpu as pltpu
from jax.sharding import PartitionSpec as P


DAMPING = 0.1
F32 = jnp.float32
BF16 = jnp.bfloat16
BOTH = ("cuts", "rows")


def host_split(table):
    high = table.astype(np.float32).astype(ml_dtypes.bfloat16)
    low = (table - high.astype(np.float64)).astype(ml_dtypes.bfloat16)
    return high, low


def dft_tables(extent):
    position = np.arange(extent)
    angle = (np.outer(position, position) % extent) * (2.0 * math.pi / extent)
    cos = np.cos(angle) / math.sqrt(extent)
    sin = np.sin(angle) / math.sqrt(extent)
    out = [*host_split(cos)]
    for imag in (-sin, sin):
        out += [*host_split(imag - cos), *host_split(cos + imag)]
    return out


def split(values):
    high = values.astype(BF16)
    low = (values - high.astype(F32)).astype(BF16)
    return high, low


def dot(first, second):
    return lax.dot_general(
        first, second, (((1,), (0,)), ((), ())), preferred_element_type=F32
    )


def by_right(values, high, low):
    vh, vl = split(values)
    return dot(vh, high) + dot(vl, high) + dot(vh, low)


def by_left(values, high, low):
    vh, vl = split(values)
    return dot(high, vh) + dot(high, vl) + dot(low, vh)


def complex_product(multiply, real, imag, t):
    shared = multiply(real + imag, t[0][...], t[1][...])
    cross_real = multiply(real, t[2][...], t[3][...])
    cross_imag = multiply(imag, t[4][...], t[5][...])
    return shared - cross_imag, shared + cross_real


def pick(tables, inverse):
    return [*tables[:2], *(tables[6:10] if inverse else tables[2:6])]


def to_lanes(values, count):
    rows = values.shape[0] // count
    return jnp.concatenate([values[c * rows : (c + 1) * rows] for c in range(count)], axis=1)


def to_rows(values, count):
    cols = values.shape[1] // count
    return jnp.concatenate([values[:, c * cols : (c + 1) * cols] for c in range(count)], axis=0)


def forward(real, imag, maps, count, tables):
    t = pick(tables, False)
    prod_real = jnp.concatenate(
        [maps[2 * c] * real - maps[2 * c + 1] * imag for c in range(count)], axis=0
    )
    prod_imag = jnp.concatenate(
        [maps[2 * c] * imag + maps[2 * c + 1] * real for c in range(count)], axis=0
    )
    re, im = complex_product(by_right, prod_real, prod_imag, t)
    return complex_product(by_left, to_lanes(re, count), to_lanes(im, count), t)


def adjoint(re, im, maps, count, tables):
    t = pick(tables, True)
    re, im = complex_product(by_left, re, im, t)
    re, im = complex_product(by_right, to_rows(re, count), to_rows(im, count), t)
    rows = re.shape[0] // count
    out_real = out_imag = 0.0
    for c in range(count):
        a, b = re[c * rows : (c + 1) * rows], im[c * rows : (c + 1) * rows]
        sr, si = maps[2 * c], maps[2 * c + 1]
        out_real = out_real + (sr * a + si * b)
        out_imag = out_imag + (sr * b - si * a)
    return out_real, out_imag


def total(values):
    return jnp.sum(jnp.sum(values, axis=0, keepdims=True), axis=1, keepdims=True)


def inner(first, second):
    return total(first[0] * second[0] + first[1] * second[1])


def normal(real, imag, maps, count, tables, wt, spec_ref, part_ref):
    re, im = forward(real, imag, maps, count, tables)
    spec_ref[0], spec_ref[1] = re, im
    wide = jnp.concatenate([wt] * count, axis=1)
    part_ref[0], part_ref[1] = adjoint(re * wide, im * wide, maps, count, tables)


def block_of(turn, half, column, blocks):
    if turn < blocks // 2:
        return turn ^ half, column
    return (turn - blocks // 2) ^ half ^ (2 - 2 * column), 1 - column


def block_row(turn, info, blocks, extent):
    column, half = info[0], info[2]
    pair = lax.bitwise_xor(jnp.int32(turn % (blocks // 2)), half)
    if turn >= blocks // 2:
        pair = lax.bitwise_xor(pair, 2 - 2 * column)
        column = 1 - column
    return pl.multiple_of((pair * 2 + column) * extent, extent)


def at_home(kernel):
    def guarded(*refs):
        @pl.when(refs[0][1] == 1)
        def _():
            kernel(*refs)

    return guarded


def first_kernel(blocks, planes, info, steep_ref, *refs):
    messages, refs = refs[:blocks], refs[blocks:]
    tables, refs = refs[:10], refs[10:]
    maps, image, wt_ref, spec_ref, part_ref, odds, sems = refs
    extent = messages[0].shape[1]
    copies = []
    for k, msg in enumerate(messages):
        rows = pl.ds(block_row(k, info, blocks, extent), extent)
        copies += [
            pltpu.make_async_copy(msg.at[:planes], maps.at[:, rows], sems.at[0, k]),
            pltpu.make_async_copy(msg.at[pl.ds(planes, 2)], image.at[:, rows], sems.at[1, k]),
            pltpu.make_async_copy(msg.at[planes + 2], odds.at[rows], sems.at[2, k]),
        ]
    for copy in copies:
        copy.start()
    for copy in copies:
        copy.wait()
    wt = jax.nn.sigmoid(steep_ref[0] * odds[...]).T
    wt_ref[...] = wt
    normal(image[0], image[1], maps, planes // 2, tables, wt, spec_ref, part_ref)


def second_kernel(info, image, part, other, maps, wt_ref, *refs):
    tables, refs = refs[:10], refs[10:]
    residual_ref, dir_ref, sc_ref, spec_ref, part_ref = refs
    u = (image[0], image[1])
    q = tuple(part[i] + other[i] + DAMPING * u[i] for i in range(2))
    norm = inner(u, u)
    alpha = norm / inner(u, q)
    r = tuple(u[i] - alpha * q[i] for i in range(2))
    norm_next = inner(r, r)
    p = tuple(r[i] + (norm_next / norm) * u[i] for i in range(2))
    for i in range(2):
        residual_ref[i] = r[i]
        dir_ref[i] = p[i]
    sc_ref[0] = jnp.broadcast_to(alpha, sc_ref.shape[1:])
    sc_ref[1] = jnp.broadcast_to(norm_next, sc_ref.shape[1:])
    normal(p[0], p[1], maps, maps.shape[0] // 2, tables, wt_ref[...], spec_ref, part_ref)


def third_kernel(blocks, planes, info, image, res_ref, dir_ref, sc_in, part, other, maps,
                 wt_ref, spec0_ref, spec1_ref, *refs):
    messages, refs = refs[:blocks], refs[blocks:]
    tables, refs = refs[:10], refs[10:]
    sol_ref, p_ref, sc_ref, out_ref, data, recon, spec0, spec1, sems = refs
    extent = messages[0].shape[1]
    copies = []
    for k, msg in enumerate(messages):
        rows = pl.ds(block_row(k, info, blocks, extent), extent)
        copies += [
            pltpu.make_async_copy(msg.at[pl.ds(planes, 2)], recon.at[:, rows], sems.at[1, k]),
            pltpu.make_async_copy(msg.at[:planes], data.at[:, rows], sems.at[0, k]),
        ]
    copies += [
        pltpu.make_async_copy(spec0_ref, spec0, sems.at[2, 0]),
        pltpu.make_async_copy(spec1_ref, spec1, sems.at[2, 1]),
    ]
    for copy in copies:
        copy.start()
    count = planes // 2
    n = image.shape[1]
    alpha0, norm = sc_in[0, :1, :1], sc_in[1, :1, :1]
    p = (dir_ref[0], dir_ref[1])
    q = tuple(part[i] + other[i] + DAMPING * p[i] for i in range(2))
    alpha1 = norm / inner(p, q)
    r = tuple(res_ref[i] - alpha1 * q[i] for i in range(2))
    norm_next = inner(r, r)
    for i in range(2):
        sol_ref[i] = alpha0 * image[i] + alpha1 * p[i]
    p = tuple(r[i] + (norm_next / norm) * p[i] for i in range(2))
    p_ref[0], p_ref[1] = p
    re, im = forward(p[0], p[1], maps, count, tables)
    wide = jnp.concatenate([wt_ref[...]] * count, axis=1)
    energy = total(wide * (re * re + im * im))
    sc_ref[0] = jnp.broadcast_to(norm_next, sc_ref.shape[1:])
    sc_ref[1] = jnp.broadcast_to(inner(p, p), sc_ref.shape[1:])
    for copy in copies:
        copy.wait()
    est_re, est_im = forward(recon[0], recon[1], maps, count, tables)
    known = last = 0.0
    for c in range(count):
        s = slice(c * n, (c + 1) * n)
        diff_re = data[2 * c].T - est_re[:, s]
        diff_im = data[2 * c + 1].T - est_im[:, s]
        sol_re = alpha0 * spec0[0, :, s] + alpha1 * spec1[0, :, s]
        sol_im = alpha0 * spec0[1, :, s] + alpha1 * spec1[1, :, s]
        known = known + (sol_re * diff_re + sol_im * diff_im)
        last = last + (re[:, s] * diff_re + im[:, s] * diff_im)
    out_ref[:n] = known
    out_ref[n : 2 * n] = last
    out_ref[2 * n :] = jnp.broadcast_to(energy, (out_ref.shape[0] - 2 * n, n))


def fourth_kernel(info, mine, other, sol, p_ref, sc, *refs):
    outs, terms = refs[:-1], refs[-1]
    half = info[2]
    n = sol.shape[1]
    extent = outs[0].shape[1]
    energy = mine[2 * n :, :][:1, :1] + other[2 * n :, :][:1, :1] + DAMPING * sc[1, :1, :1]
    alpha = sc[0, :1, :1] / energy
    terms[...] = (
        (mine[:n] + other[:n]) + alpha * (mine[n : 2 * n] + other[n : 2 * n])
    ).T
    for k, out in enumerate(outs):
        rows = pl.ds(pl.multiple_of((half * len(outs) + k) * extent, extent), extent)
        out[0] = sol[0, rows] + alpha * p_ref[0, rows]
        out[1] = sol[1, rows] + alpha * p_ref[1, rows]
        out[2] = terms[rows]


def call(*args, **kwargs):
    def run(*operands):
        return pl.pallas_call(*args, compiler_params=PARAMS, **kwargs)(*operands)

    return run


VMEM = pl.BlockSpec(memory_space=pltpu.VMEM)
SMEM = pl.BlockSpec(memory_space=pltpu.SMEM)
ANY = pl.BlockSpec(memory_space=pl.ANY)
PARAMS = pltpu.CompilerParams(vmem_limit_bytes=24 << 20)


def shape(*dims):
    return jax.ShapeDtypeStruct(dims, F32)


def home_row(piece, blocks):
    first = blocks // 4
    return first if piece % 2 == 0 else blocks - 1 - first


def detour(piece, blocks):
    return (blocks // 2 - 1) * (piece % 2)


def carrier(piece, pair, turn, blocks):
    return (piece ^ (1 - turn % 2)) * blocks + pair * 2 + piece % 2


def gather_pairs(turn, pieces, blocks, moved):
    pairs = []
    for piece in range(pieces):
        for half in range(2):
            pair, column = block_of(turn, half, piece % 2, blocks)
            source = piece * blocks + pair * 2 + column
            if column != piece % 2 and moved(piece, pair):
                source = carrier(piece, pair, turn, blocks)
            target = (piece - piece % 2 + half) * blocks + home_row(piece, blocks)
            pairs.append((source, target))
    return pairs


def move_pairs(turn, pieces, blocks, moved):
    pairs = []
    for piece in range(pieces):
        for pair in range(blocks // 2):
            if moved(piece, pair):
                source = piece * blocks + pair * 2 + 1 - piece % 2
                pairs.append((source, carrier(piece, pair, turn, blocks)))
    return pairs


def scatter_pairs(turn, pieces, blocks):
    pairs = []
    for piece in range(pieces):
        for half in range(2):
            source = (piece - piece % 2 + half) * blocks + home_row(piece, blocks)
            target = piece * blocks + turn + half * (blocks // 2)
            pairs.append((source, target))
    return pairs


def steps(
    upstream_loss_derivative,
    estimated_slice_image,
    receiver_profile_maps,
    measured_fourier_data,
    acquisition_choice_odds,
    sigmoid_steepness,
):
    blocks = lax.axis_size("rows")
    pieces = lax.axis_size("cuts")
    row = lax.axis_index("rows")
    half = lax.rem(lax.axis_index("cuts"), 2)
    column = (row == home_row(1, blocks)).astype(jnp.int32)
    home = column + (row == home_row(0, blocks)).astype(jnp.int32)
    info = jnp.stack([column, home, half]).astype(jnp.int32)
    odd = lax.rem(row // 2, 2)
    extent = upstream_loss_derivative.shape[3]
    n = upstream_loss_derivative.shape[4]
    coils = receiver_profile_maps.shape[1]
    planes = coils
    count = coils // 2
    tables = [jnp.asarray(t) for t in dft_tables(n)]
    swap = [(i, i ^ 1) for i in range(pieces)]

    maps = receiver_profile_maps.reshape(2, planes, extent, n)
    data = measured_fourier_data.reshape(2, planes, extent, n)
    upstream = upstream_loss_derivative.reshape(2, extent, n)
    recon = estimated_slice_image.reshape(2, extent, n)
    take = lambda values, i: lax.dynamic_index_in_dim(values, i, 0, keepdims=False)

    def build(values, *more):
        sends = [jnp.concatenate([take(values, i), *more], axis=0) for i in (odd, 1 - odd)]
        return lax.optimization_barrier(sends)

    def ends(piece, pair):
        return pair == detour(piece, blocks)

    def remote(piece, pair):
        return pair != home_row(piece, blocks) // 2

    def move(sends, moved):
        return [
            lax.ppermute(send, BOTH, move_pairs(i, pieces, blocks, moved))
            for i, send in enumerate(sends)
        ]

    device = lax.axis_index("cuts") * blocks + row

    def gather(sends, turns, moved, carried=None):
        got = {}
        for i in range(2):
            groups = []
            for k in [k for k in turns if k % 2 == i]:
                pairs = gather_pairs(k, pieces, blocks, moved)
                carry = {t for _, t in move_pairs(k, pieces, blocks, moved)} if carried else set()
                own = {s for s, _ in gather_pairs(k, pieces, blocks, lambda *_: False)}
                sources = {s for s, _ in pairs}
                passed, direct = (sources & carry) - (sources & own), sources & own
                for group in groups:
                    if not (group[1] | passed) & (group[2] | direct):
                        break
                else:
                    group = [[], set(), set()]
                    groups.append(group)
                group[0].append((k, pairs))
                group[1] |= passed
                group[2] |= direct
            for rounds, passed, _ in groups:
                send = sends[i]
                if passed:
                    here = functools.reduce(lambda x, t: x | (device == t), sorted(passed), False)
                    send = jnp.where(here, carried[i], send)
                got |= {k: lax.ppermute(send, BOTH, pairs) for k, pairs in rounds}
        return got

    turns = blocks // 2
    near, far = range(turns), range(turns, blocks)
    late = sorted({turns + 2, turns + 3, blocks - 2, blocks - 1})
    sends = build(maps, upstream, acquisition_choice_odds)
    first = gather(sends, [k for k in far if k not in late], ends)
    carried = move(sends, ends)
    first |= gather(sends, near, ends)
    first |= gather(sends, late, ends, carried)
    first = [first[k] for k in range(blocks)]
    sends = build(data, recon)
    carried = move(sends, remote)
    second = gather(sends, near, remote)
    second |= gather(sends, far, remote, carried)
    second = [second[k] for k in range(blocks)]

    image, spectrum = shape(2, n, n), shape(2, n, count * n)
    scalars = shape(2, 8, 128)
    stacked = shape(planes, n, n)
    maps_full, u, wt, spec0, part0 = call(
        at_home(functools.partial(first_kernel, blocks, planes)),
        in_specs=[SMEM, SMEM] + [ANY] * blocks + [VMEM] * 10,
        out_specs=[VMEM] * 5,
        out_shape=[stacked, image, shape(n, n), spectrum, image],
        scratch_shapes=[pltpu.VMEM((n, n), F32), pltpu.SemaphoreType.DMA((3, blocks))],
    )(info, sigmoid_steepness, *first, *tables)
    other0 = lax.ppermute(part0, "cuts", swap)
    res1, dir1, sc1, spec1, part1 = call(
        at_home(second_kernel),
        in_specs=[SMEM] + [VMEM] * 15,
        out_specs=[VMEM] * 5,
        out_shape=[image, image, scalars, spectrum, image],
    )(info, u, part0, other0, maps_full, wt, *tables)
    other1 = lax.ppermute(part1, "cuts", swap)
    sol2, dir2, sc2, mine = call(
        at_home(functools.partial(third_kernel, blocks, planes)),
        in_specs=[SMEM] + [VMEM] * 8 + [ANY] * 2 + [ANY] * blocks + [VMEM] * 10,
        out_specs=[VMEM] * 4,
        out_shape=[image, image, scalars, shape(2 * n + 8, n)],
        scratch_shapes=[
            pltpu.VMEM((planes, n, n), F32),
            pltpu.VMEM((2, n, n), F32),
            pltpu.VMEM((2, n, count * n), F32),
            pltpu.VMEM((2, n, count * n), F32),
            pltpu.SemaphoreType.DMA((3, blocks)),
        ],
    )(info, u, res1, dir1, sc1, part1, other1, maps_full, wt, spec0, spec1, *second, *tables)
    other = lax.ppermute(mine, "cuts", swap)
    outs = call(
        at_home(fourth_kernel),
        in_specs=[SMEM] + [VMEM] * 5,
        out_specs=[VMEM] * turns,
        out_shape=[shape(3, extent, n)] * turns,
        scratch_shapes=[pltpu.VMEM((n, n), F32)],
    )(info, mine, other, sol2, dir2, sc2)
    parts = [
        lax.ppermute(outs[k], BOTH, scatter_pairs(k, pieces, blocks)) for k in range(turns)
    ]
    whole = parts[0]
    for part in parts[1:]:
        whole = whole + part
    term = whole[2]
    step = 1
    while step < pieces:
        term = term + lax.ppermute(term, "cuts", [(i, i ^ step) for i in range(pieces)])
        step *= 2
    steep = sigmoid_steepness[0]
    weights = jax.nn.sigmoid(steep * acquisition_choice_odds)
    slices = upstream_loss_derivative.shape[0] * pieces
    gradient = steep * weights * (1.0 - weights) * term[None] / slices
    return whole[:2].reshape(upstream_loss_derivative.shape), gradient


def solution(mesh):
    return jax.shard_map(
        steps,
        mesh=mesh,
        in_specs=(
            P("cuts", None, None, "rows", None),
            P("cuts", None, None, "rows", None),
            P("cuts", None, None, "rows", None),
            P("cuts", None, None, None, "rows", None),
            P(None, "rows", None),
            P(),
        ),
        out_specs=(P("cuts", None, None, "rows", None), P(None, "rows", None)),
        check_vma=False,
    )
```

```python
import functools
import math

import jax
import jax.numpy as jnp
import ml_dtypes
import numpy as np
from jax import lax
from jax.experimental import pallas as pl
from jax.experimental.pallas import tpu as pltpu
from jax.sharding import PartitionSpec as P


DAMPING = 0.1
F32 = jnp.float32
BF16 = jnp.bfloat16
BOTH = ("cuts", "rows")


def host_split(table):
    high = table.astype(np.float32).astype(ml_dtypes.bfloat16)
    low = (table - high.astype(np.float64)).astype(ml_dtypes.bfloat16)
    return high, low


def dft_tables(extent):
    position = np.arange(extent)
    angle = (np.outer(position, position) % extent) * (2.0 * math.pi / extent)
    cos = np.cos(angle) / math.sqrt(extent)
    sin = np.sin(angle) / math.sqrt(extent)
    out = [*host_split(cos)]
    for imag in (-sin, sin):
        out += [*host_split(imag - cos), *host_split(cos + imag)]
    return out


def split(values):
    high = values.astype(BF16)
    low = (values - high.astype(F32)).astype(BF16)
    return high, low


def dot(first, second):
    return lax.dot_general(
        first, second, (((1,), (0,)), ((), ())), preferred_element_type=F32
    )


def by_right(values, high, low):
    vh, vl = split(values)
    return dot(vh, high) + dot(vl, high) + dot(vh, low)


def by_left(values, high, low):
    vh, vl = split(values)
    return dot(high, vh) + dot(high, vl) + dot(low, vh)


def complex_product(multiply, real, imag, t):
    shared = multiply(real + imag, t[0][...], t[1][...])
    cross_real = multiply(real, t[2][...], t[3][...])
    cross_imag = multiply(imag, t[4][...], t[5][...])
    return shared - cross_imag, shared + cross_real


def pick(tables, inverse):
    return [*tables[:2], *(tables[6:10] if inverse else tables[2:6])]


def to_lanes(values, count):
    rows = values.shape[0] // count
    return jnp.concatenate([values[c * rows : (c + 1) * rows] for c in range(count)], axis=1)


def to_rows(values, count):
    cols = values.shape[1] // count
    return jnp.concatenate([values[:, c * cols : (c + 1) * cols] for c in range(count)], axis=0)


def forward(real, imag, maps, count, tables):
    t = pick(tables, False)
    prod_real = jnp.concatenate(
        [maps[2 * c] * real - maps[2 * c + 1] * imag for c in range(count)], axis=0
    )
    prod_imag = jnp.concatenate(
        [maps[2 * c] * imag + maps[2 * c + 1] * real for c in range(count)], axis=0
    )
    re, im = complex_product(by_right, prod_real, prod_imag, t)
    return complex_product(by_left, to_lanes(re, count), to_lanes(im, count), t)


def adjoint(re, im, maps, count, tables):
    t = pick(tables, True)
    re, im = complex_product(by_left, re, im, t)
    re, im = complex_product(by_right, to_rows(re, count), to_rows(im, count), t)
    rows = re.shape[0] // count
    out_real = out_imag = 0.0
    for c in range(count):
        a, b = re[c * rows : (c + 1) * rows], im[c * rows : (c + 1) * rows]
        sr, si = maps[2 * c], maps[2 * c + 1]
        out_real = out_real + (sr * a + si * b)
        out_imag = out_imag + (sr * b - si * a)
    return out_real, out_imag


def total(values):
    return jnp.sum(jnp.sum(values, axis=0, keepdims=True), axis=1, keepdims=True)


def inner(first, second):
    return total(first[0] * second[0] + first[1] * second[1])


def normal(real, imag, maps, count, tables, wt, spec, part_ref, keep):
    re, im = forward(real, imag, maps, count, tables)
    spec[0], spec[1] = re, im
    keep.start()
    wide = jnp.concatenate([wt] * count, axis=1)
    part_ref[0], part_ref[1] = adjoint(re * wide, im * wide, maps, count, tables)
    keep.wait()


def block_of(turn, half, column, blocks):
    if turn < blocks // 2:
        return turn ^ half, column
    return (turn - blocks // 2) ^ half ^ (2 - 2 * column), 1 - column


def block_row(turn, info, blocks, extent):
    column, half = info[0], info[2]
    pair = lax.bitwise_xor(jnp.int32(turn % (blocks // 2)), half)
    if turn >= blocks // 2:
        pair = lax.bitwise_xor(pair, 2 - 2 * column)
        column = 1 - column
    return pl.multiple_of((pair * 2 + column) * extent, extent)


def at_home(kernel):
    def guarded(*refs):
        @pl.when(refs[0][1] == 1)
        def _():
            kernel(*refs)

    return guarded


def first_kernel(blocks, planes, info, steep_ref, *refs):
    messages, refs = refs[:blocks], refs[blocks:]
    table_ref, maps, image, wt_ref, spec_ref, part_ref, odds, tables, spec, sems = refs
    keep = pltpu.make_async_copy(spec, spec_ref, sems.at[3, 1])
    load = pltpu.make_async_copy(table_ref, tables, sems.at[3, 0])
    extent = messages[0].shape[1]
    copies = []
    for k, msg in enumerate(messages):
        rows = pl.ds(block_row(k, info, blocks, extent), extent)
        copies += [
            pltpu.make_async_copy(msg.at[:planes], maps.at[:, rows], sems.at[0, k]),
            pltpu.make_async_copy(msg.at[pl.ds(planes, 2)], image.at[:, rows], sems.at[1, k]),
            pltpu.make_async_copy(msg.at[planes + 2], odds.at[rows], sems.at[2, k]),
        ]
    for copy in (*copies, load):
        copy.start()
    for copy in (*copies, load):
        copy.wait()
    wt = jax.nn.sigmoid(steep_ref[0] * odds[...]).T
    wt_ref[...] = wt
    normal(image[0], image[1], maps, planes // 2, tables, wt, spec, part_ref, keep)


def second_kernel(info, image, part, other, maps, wt_ref, table_ref, *refs):
    residual_ref, dir_ref, sc_ref, spec_ref, part_ref, tables, spec, sems = refs
    load = pltpu.make_async_copy(table_ref, tables, sems.at[0])
    keep = pltpu.make_async_copy(spec, spec_ref, sems.at[1])
    load.start()
    u = (image[0], image[1])
    q = tuple(part[i] + other[i] + DAMPING * u[i] for i in range(2))
    norm = inner(u, u)
    alpha = norm / inner(u, q)
    r = tuple(u[i] - alpha * q[i] for i in range(2))
    norm_next = inner(r, r)
    p = tuple(r[i] + (norm_next / norm) * u[i] for i in range(2))
    for i in range(2):
        residual_ref[i] = r[i]
        dir_ref[i] = p[i]
    sc_ref[0] = jnp.broadcast_to(alpha, sc_ref.shape[1:])
    sc_ref[1] = jnp.broadcast_to(norm_next, sc_ref.shape[1:])
    load.wait()
    normal(p[0], p[1], maps, maps.shape[0] // 2, tables, wt_ref[...], spec, part_ref, keep)


def third_kernel(blocks, planes, info, image, res_ref, dir_ref, sc_in, part, other, maps,
                 wt_ref, spec0_ref, spec1_ref, *refs):
    messages, refs = refs[:blocks], refs[blocks:]
    table_ref, sol_ref, p_ref, sc_ref, out_ref, data, recon, spec0, spec1, tables, sems = refs
    load = pltpu.make_async_copy(table_ref, tables, sems.at[2, 2])
    load.start()
    extent = messages[0].shape[1]
    copies = []
    for k, msg in enumerate(messages):
        rows = pl.ds(block_row(k, info, blocks, extent), extent)
        copies += [
            pltpu.make_async_copy(msg.at[pl.ds(planes, 2)], recon.at[:, rows], sems.at[1, k]),
            pltpu.make_async_copy(msg.at[:planes], data.at[:, rows], sems.at[0, k]),
        ]
    copies += [
        pltpu.make_async_copy(spec0_ref, spec0, sems.at[2, 0]),
        pltpu.make_async_copy(spec1_ref, spec1, sems.at[2, 1]),
    ]
    for copy in copies:
        copy.start()
    count = planes // 2
    n = image.shape[1]
    alpha0, norm = sc_in[0, :1, :1], sc_in[1, :1, :1]
    p = (dir_ref[0], dir_ref[1])
    q = tuple(part[i] + other[i] + DAMPING * p[i] for i in range(2))
    alpha1 = norm / inner(p, q)
    r = tuple(res_ref[i] - alpha1 * q[i] for i in range(2))
    norm_next = inner(r, r)
    for i in range(2):
        sol_ref[i] = alpha0 * image[i] + alpha1 * p[i]
    p = tuple(r[i] + (norm_next / norm) * p[i] for i in range(2))
    p_ref[0], p_ref[1] = p
    load.wait()
    re, im = forward(p[0], p[1], maps, count, tables)
    wide = jnp.concatenate([wt_ref[...]] * count, axis=1)
    energy = total(wide * (re * re + im * im))
    sc_ref[0] = jnp.broadcast_to(norm_next, sc_ref.shape[1:])
    sc_ref[1] = jnp.broadcast_to(inner(p, p), sc_ref.shape[1:])
    for copy in copies:
        copy.wait()
    est_re, est_im = forward(recon[0], recon[1], maps, count, tables)
    known = last = 0.0
    for c in range(count):
        s = slice(c * n, (c + 1) * n)
        diff_re = data[2 * c].T - est_re[:, s]
        diff_im = data[2 * c + 1].T - est_im[:, s]
        sol_re = alpha0 * spec0[0, :, s] + alpha1 * spec1[0, :, s]
        sol_im = alpha0 * spec0[1, :, s] + alpha1 * spec1[1, :, s]
        known = known + (sol_re * diff_re + sol_im * diff_im)
        last = last + (re[:, s] * diff_re + im[:, s] * diff_im)
    out_ref[:n] = known
    out_ref[n : 2 * n] = last
    out_ref[2 * n :] = jnp.broadcast_to(energy, (out_ref.shape[0] - 2 * n, n))


def fourth_kernel(info, mine, other, sol, p_ref, sc, *refs):
    outs, terms = refs[:-1], refs[-1]
    half = info[2]
    n = sol.shape[1]
    extent = outs[0].shape[1]
    energy = mine[2 * n :, :][:1, :1] + other[2 * n :, :][:1, :1] + DAMPING * sc[1, :1, :1]
    alpha = sc[0, :1, :1] / energy
    terms[...] = (
        (mine[:n] + other[:n]) + alpha * (mine[n : 2 * n] + other[n : 2 * n])
    ).T
    for k, out in enumerate(outs):
        rows = pl.ds(pl.multiple_of((half * len(outs) + k) * extent, extent), extent)
        out[0] = sol[0, rows] + alpha * p_ref[0, rows]
        out[1] = sol[1, rows] + alpha * p_ref[1, rows]
        out[2] = terms[rows]


def call(*args, **kwargs):
    def run(*operands):
        return pl.pallas_call(*args, compiler_params=PARAMS, **kwargs)(*operands)

    return run


VMEM = pl.BlockSpec(memory_space=pltpu.VMEM)
SMEM = pl.BlockSpec(memory_space=pltpu.SMEM)
HBM = pl.BlockSpec(memory_space=pltpu.HBM)
PARAMS = pltpu.CompilerParams(vmem_limit_bytes=20 << 20)


def in_hbm(values):
    return pltpu.with_memory_space_constraint(values, pltpu.HBM)


def shape(*dims):
    return jax.ShapeDtypeStruct(dims, F32)


def home_row(piece, blocks):
    first = blocks // 4
    return first if piece % 2 == 0 else blocks - 1 - first


def detour(piece, blocks):
    return (blocks // 2 - 1) * (piece % 2)


def carrier(piece, pair, turn, blocks):
    return (piece ^ (1 - turn % 2)) * blocks + pair * 2 + piece % 2


def gather_pairs(turn, pieces, blocks, moved):
    pairs = []
    for piece in range(pieces):
        for half in range(2):
            pair, column = block_of(turn, half, piece % 2, blocks)
            source = piece * blocks + pair * 2 + column
            if column != piece % 2 and moved(piece, pair):
                source = carrier(piece, pair, turn, blocks)
            target = (piece - piece % 2 + half) * blocks + home_row(piece, blocks)
            pairs.append((source, target))
    return pairs


def move_pairs(turn, pieces, blocks, moved):
    pairs = []
    for piece in range(pieces):
        for pair in range(blocks // 2):
            if moved(piece, pair):
                source = piece * blocks + pair * 2 + 1 - piece % 2
                pairs.append((source, carrier(piece, pair, turn, blocks)))
    return pairs


def scatter_pairs(turn, pieces, blocks):
    pairs = []
    for piece in range(pieces):
        for half in range(2):
            source = (piece - piece % 2 + half) * blocks + home_row(piece, blocks)
            target = piece * blocks + turn + half * (blocks // 2)
            pairs.append((source, target))
    return pairs


def steps(
    upstream_loss_derivative,
    estimated_slice_image,
    receiver_profile_maps,
    measured_fourier_data,
    acquisition_choice_odds,
    sigmoid_steepness,
):
    blocks = lax.axis_size("rows")
    pieces = lax.axis_size("cuts")
    row = lax.axis_index("rows")
    half = lax.rem(lax.axis_index("cuts"), 2)
    column = (row == home_row(1, blocks)).astype(jnp.int32)
    home = column + (row == home_row(0, blocks)).astype(jnp.int32)
    info = jnp.stack([column, home, half]).astype(jnp.int32)
    odd = lax.rem(row // 2, 2)
    extent = upstream_loss_derivative.shape[3]
    n = upstream_loss_derivative.shape[4]
    coils = receiver_profile_maps.shape[1]
    planes = coils
    count = coils // 2
    tables = jnp.asarray(np.stack(dft_tables(n)))
    table_space = pltpu.VMEM(tables.shape, BF16)
    spec_space = pltpu.VMEM((2, n, count * n), F32)
    swap = [(i, i ^ 1) for i in range(pieces)]

    maps = receiver_profile_maps.reshape(2, planes, extent, n)
    data = measured_fourier_data.reshape(2, planes, extent, n)
    upstream = upstream_loss_derivative.reshape(2, extent, n)
    recon = estimated_slice_image.reshape(2, extent, n)
    take = lambda values, i: lax.dynamic_index_in_dim(values, i, 0, keepdims=False)

    def build(values, *more):
        sends = [jnp.concatenate([take(values, i), *more], axis=0) for i in (odd, 1 - odd)]
        return lax.optimization_barrier(sends)

    def ends(piece, pair):
        return pair == detour(piece, blocks)

    def remote(piece, pair):
        return pair != home_row(piece, blocks) // 2

    def move(sends, moved):
        return [
            lax.ppermute(send, BOTH, move_pairs(i, pieces, blocks, moved))
            for i, send in enumerate(sends)
        ]

    device = lax.axis_index("cuts") * blocks + row

    def gather(sends, turns, moved, carried=None):
        got = {}
        for i in range(2):
            groups = []
            for k in [k for k in turns if k % 2 == i]:
                pairs = gather_pairs(k, pieces, blocks, moved)
                carry = {t for _, t in move_pairs(k, pieces, blocks, moved)} if carried else set()
                own = {s for s, _ in gather_pairs(k, pieces, blocks, lambda *_: False)}
                sources = {s for s, _ in pairs}
                passed, direct = (sources & carry) - (sources & own), sources & own
                for group in groups:
                    if not (group[1] | passed) & (group[2] | direct):
                        break
                else:
                    group = [[], set(), set()]
                    groups.append(group)
                group[0].append((k, pairs))
                group[1] |= passed
                group[2] |= direct
            for rounds, passed, _ in groups:
                send = sends[i]
                if passed:
                    here = functools.reduce(lambda x, t: x | (device == t), sorted(passed), False)
                    send = jnp.where(here, carried[i], send)
                got |= {k: lax.ppermute(send, BOTH, pairs) for k, pairs in rounds}
        return got

    turns = blocks // 2
    near, far = range(turns), range(turns, blocks)
    late = sorted({turns + 2, turns + 3, blocks - 2, blocks - 1})
    sends = build(maps, upstream, acquisition_choice_odds)
    first = gather(sends, [k for k in far if k not in late], ends)
    carried = move(sends, ends)
    first |= gather(sends, near, ends)
    first |= gather(sends, late, ends, carried)
    first = [in_hbm(first[k]) for k in range(blocks)]
    sends = build(data, recon)
    carried = move(sends, remote)
    second = gather(sends, near, remote)
    second |= gather(sends, far, remote, carried)
    second = [in_hbm(second[k]) for k in range(blocks)]

    image, spectrum = shape(2, n, n), shape(2, n, count * n)
    scalars = shape(2, 8, 128)
    stacked = shape(planes, n, n)
    maps_full, u, wt, spec0, part0 = call(
        at_home(functools.partial(first_kernel, blocks, planes)),
        in_specs=[SMEM, SMEM] + [HBM] * (blocks + 1),
        out_specs=[VMEM] * 3 + [HBM] + [VMEM],
        out_shape=[stacked, image, shape(n, n), spectrum, image],
        scratch_shapes=[
            pltpu.VMEM((n, n), F32),
            table_space,
            spec_space,
            pltpu.SemaphoreType.DMA((4, blocks)),
        ],
    )(info, sigmoid_steepness, *first, tables)
    u, wt, spec0 = in_hbm(u), in_hbm(wt), in_hbm(spec0)
    other0 = lax.ppermute(part0, "cuts", swap)
    res1, dir1, sc1, spec1, part1 = call(
        at_home(second_kernel),
        in_specs=[SMEM] + [VMEM] * 5 + [HBM],
        out_specs=[VMEM] * 3 + [HBM] + [VMEM],
        out_shape=[image, image, scalars, spectrum, image],
        scratch_shapes=[table_space, spec_space, pltpu.SemaphoreType.DMA((2,))],
    )(info, u, part0, other0, maps_full, wt, tables)
    spec1 = in_hbm(spec1)
    other1 = lax.ppermute(part1, "cuts", swap)
    sol2, dir2, sc2, mine = call(
        at_home(functools.partial(third_kernel, blocks, planes)),
        in_specs=[SMEM] + [VMEM] * 8 + [HBM] * (blocks + 3),
        out_specs=[VMEM] * 4,
        out_shape=[image, image, scalars, shape(2 * n + 8, n)],
        scratch_shapes=[
            pltpu.VMEM((planes, n, n), F32),
            pltpu.VMEM((2, n, n), F32),
            spec_space,
            spec_space,
            table_space,
            pltpu.SemaphoreType.DMA((3, blocks)),
        ],
    )(info, u, res1, dir1, sc1, part1, other1, maps_full, wt, spec0, spec1, *second, tables)
    other = lax.ppermute(mine, "cuts", swap)
    outs = call(
        at_home(fourth_kernel),
        in_specs=[SMEM] + [VMEM] * 5,
        out_specs=[VMEM] * turns,
        out_shape=[shape(3, extent, n)] * turns,
        scratch_shapes=[pltpu.VMEM((n, n), F32)],
    )(info, mine, other, sol2, dir2, sc2)
    parts = [
        lax.ppermute(outs[k], BOTH, scatter_pairs(k, pieces, blocks)) for k in range(turns)
    ]
    whole = parts[0]
    for part in parts[1:]:
        whole = whole + part
    term = whole[2]
    step = 1
    while step < pieces:
        term = term + lax.ppermute(term, "cuts", [(i, i ^ step) for i in range(pieces)])
        step *= 2
    steep = sigmoid_steepness[0]
    weights = jax.nn.sigmoid(steep * acquisition_choice_odds)
    slices = upstream_loss_derivative.shape[0] * pieces
    gradient = steep * weights * (1.0 - weights) * term[None] / slices
    return whole[:2].reshape(upstream_loss_derivative.shape), gradient


def solution(mesh):
    return jax.shard_map(
        steps,
        mesh=mesh,
        in_specs=(
            P("cuts", None, None, "rows", None),
            P("cuts", None, None, "rows", None),
            P("cuts", None, None, "rows", None),
            P("cuts", None, None, None, "rows", None),
            P(None, "rows", None),
            P(),
        ),
        out_specs=(P("cuts", None, None, "rows", None), P(None, "rows", None)),
        check_vma=False,
    )
```

```python
import functools
import math

import jax
import jax.numpy as jnp
import ml_dtypes
import numpy as np
from jax import lax
from jax.experimental import pallas as pl
from jax.experimental.pallas import tpu as pltpu
from jax.sharding import PartitionSpec as P


DAMPING = 0.1
F32 = jnp.float32
BF16 = jnp.bfloat16
BOTH = ("cuts", "rows")


def host_split(table):
    high = table.astype(np.float32).astype(ml_dtypes.bfloat16)
    low = (table - high.astype(np.float64)).astype(ml_dtypes.bfloat16)
    return high, low


def dft_tables(extent):
    position = np.arange(extent)
    angle = (np.outer(position, position) % extent) * (2.0 * math.pi / extent)
    cos = np.cos(angle) / math.sqrt(extent)
    sin = np.sin(angle) / math.sqrt(extent)
    out = [*host_split(cos)]
    for imag in (-sin, sin):
        out += [*host_split(imag - cos), *host_split(cos + imag)]
    return out


def split(values):
    high = values.astype(BF16)
    low = (values - high.astype(F32)).astype(BF16)
    return high, low


def dot(first, second):
    return lax.dot_general(
        first, second, (((1,), (0,)), ((), ())), preferred_element_type=F32
    )


def by_right(values, high, low):
    vh, vl = split(values)
    return dot(vh, high) + dot(vl, high) + dot(vh, low)


def by_left(values, high, low):
    vh, vl = split(values)
    return dot(high, vh) + dot(high, vl) + dot(low, vh)


def complex_product(multiply, real, imag, t):
    shared = multiply(real + imag, t[0][...], t[1][...])
    cross_real = multiply(real, t[2][...], t[3][...])
    cross_imag = multiply(imag, t[4][...], t[5][...])
    return shared - cross_imag, shared + cross_real


def pick(tables, inverse):
    return [*tables[:2], *(tables[6:10] if inverse else tables[2:6])]


def to_lanes(values, count):
    rows = values.shape[0] // count
    return jnp.concatenate([values[c * rows : (c + 1) * rows] for c in range(count)], axis=1)


def to_rows(values, count):
    cols = values.shape[1] // count
    return jnp.concatenate([values[:, c * cols : (c + 1) * cols] for c in range(count)], axis=0)


def forward(real, imag, maps, count, tables):
    t = pick(tables, False)
    prod_real = jnp.concatenate(
        [maps[2 * c] * real - maps[2 * c + 1] * imag for c in range(count)], axis=0
    )
    prod_imag = jnp.concatenate(
        [maps[2 * c] * imag + maps[2 * c + 1] * real for c in range(count)], axis=0
    )
    re, im = complex_product(by_right, prod_real, prod_imag, t)
    return complex_product(by_left, to_lanes(re, count), to_lanes(im, count), t)


def adjoint(re, im, maps, count, tables):
    t = pick(tables, True)
    re, im = complex_product(by_left, re, im, t)
    re, im = complex_product(by_right, to_rows(re, count), to_rows(im, count), t)
    rows = re.shape[0] // count
    out_real = out_imag = 0.0
    for c in range(count):
        a, b = re[c * rows : (c + 1) * rows], im[c * rows : (c + 1) * rows]
        sr, si = maps[2 * c], maps[2 * c + 1]
        out_real = out_real + (sr * a + si * b)
        out_imag = out_imag + (sr * b - si * a)
    return out_real, out_imag


def total(values):
    return jnp.sum(jnp.sum(values, axis=0, keepdims=True), axis=1, keepdims=True)


def inner(first, second):
    return total(first[0] * second[0] + first[1] * second[1])


def normal(real, imag, maps, count, tables, wt, spec, part_ref, keep):
    re, im = forward(real, imag, maps, count, tables)
    spec[0], spec[1] = re, im
    keep.start()
    wide = jnp.concatenate([wt] * count, axis=1)
    part_ref[0], part_ref[1] = adjoint(re * wide, im * wide, maps, count, tables)
    keep.wait()


def block_of(turn, half, column, blocks):
    if turn < blocks // 2:
        return turn ^ half, column
    return (turn - blocks // 2) ^ half ^ (2 - 2 * column), 1 - column


def block_row(turn, info, blocks, extent):
    column, half = info[0], info[2]
    pair = lax.bitwise_xor(jnp.int32(turn % (blocks // 2)), half)
    if turn >= blocks // 2:
        pair = lax.bitwise_xor(pair, 2 - 2 * column)
        column = 1 - column
    return pl.multiple_of((pair * 2 + column) * extent, extent)


def at_home(kernel):
    def guarded(*refs):
        @pl.when(refs[0][1] == 1)
        def _():
            kernel(*refs)

    return guarded


def first_kernel(blocks, planes, info, steep_ref, *refs):
    messages, refs = refs[:blocks], refs[blocks:]
    table_ref, maps, image, wt_ref, spec_ref, part_ref, odds, tables, spec, sems = refs
    keep = pltpu.make_async_copy(spec, spec_ref, sems.at[3, 1])
    load = pltpu.make_async_copy(table_ref, tables, sems.at[3, 0])
    extent = messages[0].shape[1]
    copies = []
    for k, msg in enumerate(messages):
        rows = pl.ds(block_row(k, info, blocks, extent), extent)
        copies += [
            pltpu.make_async_copy(msg.at[:planes], maps.at[:, rows], sems.at[0, k]),
            pltpu.make_async_copy(msg.at[pl.ds(planes, 2)], image.at[:, rows], sems.at[1, k]),
            pltpu.make_async_copy(msg.at[planes + 2], odds.at[rows], sems.at[2, k]),
        ]
    for copy in (*copies, load):
        copy.start()
    for copy in (*copies, load):
        copy.wait()
    wt = jax.nn.sigmoid(steep_ref[0] * odds[...]).T
    wt_ref[...] = wt
    normal(image[0], image[1], maps, planes // 2, tables, wt, spec, part_ref, keep)


def second_kernel(info, image, part, other, maps, wt_ref, table_ref, *refs):
    residual_ref, dir_ref, sc_ref, spec_ref, part_ref, tables, spec, sems = refs
    load = pltpu.make_async_copy(table_ref, tables, sems.at[0])
    keep = pltpu.make_async_copy(spec, spec_ref, sems.at[1])
    load.start()
    u = (image[0], image[1])
    q = tuple(part[i] + other[i] + DAMPING * u[i] for i in range(2))
    norm = inner(u, u)
    alpha = norm / inner(u, q)
    r = tuple(u[i] - alpha * q[i] for i in range(2))
    norm_next = inner(r, r)
    p = tuple(r[i] + (norm_next / norm) * u[i] for i in range(2))
    for i in range(2):
        residual_ref[i] = r[i]
        dir_ref[i] = p[i]
    sc_ref[0] = jnp.broadcast_to(alpha, sc_ref.shape[1:])
    sc_ref[1] = jnp.broadcast_to(norm_next, sc_ref.shape[1:])
    load.wait()
    normal(p[0], p[1], maps, maps.shape[0] // 2, tables, wt_ref[...], spec, part_ref, keep)


def third_kernel(blocks, planes, info, image, res_ref, dir_ref, sc_in, part, other, maps,
                 wt_ref, spec0_ref, spec1_ref, *refs):
    messages, refs = refs[:blocks], refs[blocks:]
    table_ref, sol_ref, p_ref, sc_ref, out_ref, data, recon, spec0, spec1, tables, sems = refs
    load = pltpu.make_async_copy(table_ref, tables, sems.at[2, 2])
    load.start()
    extent = messages[0].shape[1]
    copies = []
    for k, msg in enumerate(messages):
        rows = pl.ds(block_row(k, info, blocks, extent), extent)
        copies += [
            pltpu.make_async_copy(msg.at[pl.ds(planes, 2)], recon.at[:, rows], sems.at[1, k]),
            pltpu.make_async_copy(msg.at[:planes], data.at[:, rows], sems.at[0, k]),
        ]
    copies += [
        pltpu.make_async_copy(spec0_ref, spec0, sems.at[2, 0]),
        pltpu.make_async_copy(spec1_ref, spec1, sems.at[2, 1]),
    ]
    for copy in copies:
        copy.start()
    count = planes // 2
    n = image.shape[1]
    alpha0, norm = sc_in[0, :1, :1], sc_in[1, :1, :1]
    p = (dir_ref[0], dir_ref[1])
    q = tuple(part[i] + other[i] + DAMPING * p[i] for i in range(2))
    alpha1 = norm / inner(p, q)
    r = tuple(res_ref[i] - alpha1 * q[i] for i in range(2))
    norm_next = inner(r, r)
    for i in range(2):
        sol_ref[i] = alpha0 * image[i] + alpha1 * p[i]
    p = tuple(r[i] + (norm_next / norm) * p[i] for i in range(2))
    p_ref[0], p_ref[1] = p
    load.wait()
    re, im = forward(p[0], p[1], maps, count, tables)
    wide = jnp.concatenate([wt_ref[...]] * count, axis=1)
    energy = total(wide * (re * re + im * im))
    sc_ref[0] = jnp.broadcast_to(norm_next, sc_ref.shape[1:])
    sc_ref[1] = jnp.broadcast_to(inner(p, p), sc_ref.shape[1:])
    for copy in copies:
        copy.wait()
    est_re, est_im = forward(recon[0], recon[1], maps, count, tables)
    known = last = 0.0
    for c in range(count):
        s = slice(c * n, (c + 1) * n)
        diff_re = data[2 * c].T - est_re[:, s]
        diff_im = data[2 * c + 1].T - est_im[:, s]
        sol_re = alpha0 * spec0[0, :, s] + alpha1 * spec1[0, :, s]
        sol_im = alpha0 * spec0[1, :, s] + alpha1 * spec1[1, :, s]
        known = known + (sol_re * diff_re + sol_im * diff_im)
        last = last + (re[:, s] * diff_re + im[:, s] * diff_im)
    out_ref[:n] = known
    out_ref[n : 2 * n] = last
    out_ref[2 * n :] = jnp.broadcast_to(energy, (out_ref.shape[0] - 2 * n, n))


def fourth_kernel(info, mine, other, sol, p_ref, sc, *refs):
    outs, terms = refs[:-1], refs[-1]
    half = info[2]
    n = sol.shape[1]
    extent = outs[0].shape[1]
    energy = mine[2 * n :, :][:1, :1] + other[2 * n :, :][:1, :1] + DAMPING * sc[1, :1, :1]
    alpha = sc[0, :1, :1] / energy
    terms[...] = (
        (mine[:n] + other[:n]) + alpha * (mine[n : 2 * n] + other[n : 2 * n])
    ).T
    for k, out in enumerate(outs):
        rows = pl.ds(pl.multiple_of((half * len(outs) + k) * extent, extent), extent)
        out[0] = sol[0, rows] + alpha * p_ref[0, rows]
        out[1] = sol[1, rows] + alpha * p_ref[1, rows]
        out[2] = terms[rows]


def call(*args, **kwargs):
    def run(*operands):
        return pl.pallas_call(*args, compiler_params=PARAMS, **kwargs)(*operands)

    return run


VMEM = pl.BlockSpec(memory_space=pltpu.VMEM)
SMEM = pl.BlockSpec(memory_space=pltpu.SMEM)
HBM = pl.BlockSpec(memory_space=pltpu.HBM)
PARAMS = pltpu.CompilerParams(vmem_limit_bytes=20 << 20)


def in_hbm(values):
    return pltpu.with_memory_space_constraint(values, pltpu.HBM)


def shape(*dims):
    return jax.ShapeDtypeStruct(dims, F32)


def home_row(piece, blocks):
    first = blocks // 4
    return first if piece % 2 == 0 else blocks - 1 - first


def detour(piece, blocks):
    return (blocks // 2 - 1) * (piece % 2)


def carrier(piece, pair, turn, blocks):
    return (piece ^ (1 - turn % 2)) * blocks + pair * 2 + piece % 2


def gather_pairs(turn, pieces, blocks, moved):
    pairs = []
    for piece in range(pieces):
        for half in range(2):
            pair, column = block_of(turn, half, piece % 2, blocks)
            source = piece * blocks + pair * 2 + column
            if column != piece % 2 and moved(piece, pair):
                source = carrier(piece, pair, turn, blocks)
            target = (piece - piece % 2 + half) * blocks + home_row(piece, blocks)
            pairs.append((source, target))
    return pairs


def move_pairs(turn, pieces, blocks, moved):
    pairs = []
    for piece in range(pieces):
        for pair in range(blocks // 2):
            if moved(piece, pair):
                source = piece * blocks + pair * 2 + 1 - piece % 2
                pairs.append((source, carrier(piece, pair, turn, blocks)))
    return pairs


def scatter_pairs(turn, pieces, blocks):
    pairs = []
    for piece in range(pieces):
        for half in range(2):
            source = (piece - piece % 2 + half) * blocks + home_row(piece, blocks)
            target = piece * blocks + turn + half * (blocks // 2)
            pairs.append((source, target))
    return pairs


def steps(
    upstream_loss_derivative,
    estimated_slice_image,
    receiver_profile_maps,
    measured_fourier_data,
    acquisition_choice_odds,
    sigmoid_steepness,
):
    blocks = lax.axis_size("rows")
    pieces = lax.axis_size("cuts")
    row = lax.axis_index("rows")
    half = lax.rem(lax.axis_index("cuts"), 2)
    column = (row == home_row(1, blocks)).astype(jnp.int32)
    home = column + (row == home_row(0, blocks)).astype(jnp.int32)
    info = jnp.stack([column, home, half]).astype(jnp.int32)
    odd = lax.rem(row // 2, 2)
    extent = upstream_loss_derivative.shape[3]
    n = upstream_loss_derivative.shape[4]
    coils = receiver_profile_maps.shape[1]
    planes = coils
    count = coils // 2
    tables = jnp.asarray(np.stack(dft_tables(n)))
    table_space = pltpu.VMEM(tables.shape, BF16)
    spec_space = pltpu.VMEM((2, n, count * n), F32)
    swap = [(i, i ^ 1) for i in range(pieces)]

    maps = receiver_profile_maps.reshape(2, planes, extent, n)
    data = measured_fourier_data.reshape(2, planes, extent, n)
    upstream = upstream_loss_derivative.reshape(2, extent, n)
    recon = estimated_slice_image.reshape(2, extent, n)
    take = lambda values, i: lax.dynamic_index_in_dim(values, i, 0, keepdims=False)

    def build(values, *more):
        sends = [jnp.concatenate([take(values, i), *more], axis=0) for i in (odd, 1 - odd)]
        return lax.optimization_barrier(sends)

    def ends(piece, pair):
        return pair == detour(piece, blocks)

    def remote(piece, pair):
        return all(pair != home_row(i, blocks) // 2 for i in range(2))

    def move(sends, moved):
        return [
            lax.ppermute(send, BOTH, move_pairs(i, pieces, blocks, moved))
            for i, send in enumerate(sends)
        ]

    device = lax.axis_index("cuts") * blocks + row

    def passing(sends, turns, moved, carried=None):
        out = []
        for i in range(2):
            groups = []
            for k in [k for k in turns if k % 2 == i]:
                pairs = gather_pairs(k, pieces, blocks, moved)
                carry = {t for _, t in move_pairs(k, pieces, blocks, moved)} if carried else set()
                own = {s for s, _ in gather_pairs(k, pieces, blocks, lambda *_: False)}
                sources = {s for s, _ in pairs}
                passed, direct = (sources & carry) - (sources & own), sources & own
                for group in groups:
                    if not (group[1] | passed) & (group[2] | direct):
                        break
                else:
                    group = [[], set(), set()]
                    groups.append(group)
                group[0].append((k, pairs))
                group[1] |= passed
                group[2] |= direct
            for rounds, passed, _ in groups:
                send = sends[i]
                if passed:
                    here = functools.reduce(lambda x, t: x | (device == t), sorted(passed), False)
                    send = jnp.where(here, carried[i], send)
                out.append((send, rounds))
        return out

    def gather(sends, turns, moved, carried=None):
        got = {}
        for send, rounds in passing(sends, turns, moved, carried):
            got |= {k: lax.ppermute(send, BOTH, pairs) for k, pairs in rounds}
        return got

    turns = blocks // 2
    near, far = range(turns), range(turns, blocks)
    late = sorted({turns + 2, turns + 3, blocks - 2, blocks - 1})
    sends = build(maps, upstream, acquisition_choice_odds)
    first = gather(sends, [k for k in far if k not in late], ends)
    carried = move(sends, ends)
    first |= gather(sends, near, ends)
    first |= gather(sends, late, ends, carried)
    first = [in_hbm(first[k]) for k in range(blocks)]
    sends = build(data, recon)
    carried = move(sends, remote)
    second = gather(sends, near, remote)
    sends = passing(sends, far, remote, carried)
    ready = lax.optimization_barrier((info, *[send for send, _ in sends]))
    info, sends = ready[0], [(send, rounds) for send, (_, rounds) in zip(ready[1:], sends)]
    for send, rounds in sends:
        second |= {k: lax.ppermute(send, BOTH, pairs) for k, pairs in rounds}
    second = [second[k] for k in range(blocks)]

    image, spectrum = shape(2, n, n), shape(2, n, count * n)
    scalars = shape(2, 8, 128)
    stacked = shape(planes, n, n)
    maps_full, u, wt, spec0, part0 = call(
        at_home(functools.partial(first_kernel, blocks, planes)),
        in_specs=[SMEM, SMEM] + [HBM] * (blocks + 1),
        out_specs=[VMEM] * 3 + [HBM] + [VMEM],
        out_shape=[stacked, image, shape(n, n), spectrum, image],
        scratch_shapes=[
            pltpu.VMEM((n, n), F32),
            table_space,
            spec_space,
            pltpu.SemaphoreType.DMA((4, blocks)),
        ],
    )(info, sigmoid_steepness, *first, tables)
    other0 = lax.ppermute(part0, "cuts", swap)
    res1, dir1, sc1, spec1, part1 = call(
        at_home(second_kernel),
        in_specs=[SMEM] + [VMEM] * 5 + [HBM],
        out_specs=[VMEM] * 3 + [HBM] + [VMEM],
        out_shape=[image, image, scalars, spectrum, image],
        scratch_shapes=[table_space, spec_space, pltpu.SemaphoreType.DMA((2,))],
    )(info, u, part0, other0, maps_full, wt, tables)
    other1 = lax.ppermute(part1, "cuts", swap)
    sol2, dir2, sc2, mine = call(
        at_home(functools.partial(third_kernel, blocks, planes)),
        in_specs=[SMEM] + [VMEM] * 8 + [HBM] * (blocks + 3),
        out_specs=[VMEM] * 4,
        out_shape=[image, image, scalars, shape(2 * n + 8, n)],
        scratch_shapes=[
            pltpu.VMEM((planes, n, n), F32),
            pltpu.VMEM((2, n, n), F32),
            spec_space,
            spec_space,
            table_space,
            pltpu.SemaphoreType.DMA((3, blocks)),
        ],
    )(info, u, res1, dir1, sc1, part1, other1, maps_full, wt, spec0, spec1, *second, tables)
    other = lax.ppermute(mine, "cuts", swap)
    outs = call(
        at_home(fourth_kernel),
        in_specs=[SMEM] + [VMEM] * 5,
        out_specs=[VMEM] * turns,
        out_shape=[shape(3, extent, n)] * turns,
        scratch_shapes=[pltpu.VMEM((n, n), F32)],
    )(info, mine, other, sol2, dir2, sc2)
    parts = [
        lax.ppermute(outs[k], BOTH, scatter_pairs(k, pieces, blocks)) for k in range(turns)
    ]
    whole = parts[0]
    for part in parts[1:]:
        whole = whole + part
    term = whole[2]
    step = 1
    while step < pieces:
        term = term + lax.ppermute(term, "cuts", [(i, i ^ step) for i in range(pieces)])
        step *= 2
    steep = sigmoid_steepness[0]
    weights = jax.nn.sigmoid(steep * acquisition_choice_odds)
    slices = upstream_loss_derivative.shape[0] * pieces
    gradient = steep * weights * (1.0 - weights) * term[None] / slices
    return whole[:2].reshape(upstream_loss_derivative.shape), gradient


def solution(mesh):
    return jax.shard_map(
        steps,
        mesh=mesh,
        in_specs=(
            P("cuts", None, None, "rows", None),
            P("cuts", None, None, "rows", None),
            P("cuts", None, None, "rows", None),
            P("cuts", None, None, None, "rows", None),
            P(None, "rows", None),
            P(),
        ),
        out_specs=(P("cuts", None, None, "rows", None), P(None, "rows", None)),
        check_vma=False,
    )
```

```python
import functools
import math

import jax
import jax.numpy as jnp
import ml_dtypes
import numpy as np
from jax import lax
from jax.experimental import pallas as pl
from jax.experimental.pallas import tpu as pltpu
from jax.sharding import PartitionSpec as P


DAMPING = 0.1
F32 = jnp.float32
BF16 = jnp.bfloat16
BOTH = ("cuts", "rows")


def host_split(table):
    high = table.astype(np.float32).astype(ml_dtypes.bfloat16)
    low = (table - high.astype(np.float64)).astype(ml_dtypes.bfloat16)
    return high, low


def dft_tables(extent):
    position = np.arange(extent)
    angle = (np.outer(position, position) % extent) * (2.0 * math.pi / extent)
    cos = np.cos(angle) / math.sqrt(extent)
    sin = np.sin(angle) / math.sqrt(extent)
    out = [*host_split(cos)]
    for imag in (-sin, sin):
        out += [*host_split(imag - cos), *host_split(cos + imag)]
    return out


def split(values):
    high = values.astype(BF16)
    low = (values - high.astype(F32)).astype(BF16)
    return high, low


def dot(first, second):
    return lax.dot_general(
        first, second, (((1,), (0,)), ((), ())), preferred_element_type=F32
    )


def by_right(values, high, low):
    vh, vl = split(values)
    return dot(vh, high) + dot(vl, high) + dot(vh, low)


def by_left(values, high, low):
    vh, vl = split(values)
    return dot(high, vh) + dot(high, vl) + dot(low, vh)


def complex_product(multiply, real, imag, t):
    shared = multiply(real + imag, t[0][...], t[1][...])
    cross_real = multiply(real, t[2][...], t[3][...])
    cross_imag = multiply(imag, t[4][...], t[5][...])
    return shared - cross_imag, shared + cross_real


def pick(tables, inverse):
    return [*tables[:2], *(tables[6:10] if inverse else tables[2:6])]


def to_lanes(values, count):
    rows = values.shape[0] // count
    return jnp.concatenate([values[c * rows : (c + 1) * rows] for c in range(count)], axis=1)


def to_rows(values, count):
    cols = values.shape[1] // count
    return jnp.concatenate([values[:, c * cols : (c + 1) * cols] for c in range(count)], axis=0)


def forward(real, imag, maps, count, tables):
    t = pick(tables, False)
    prod_real = jnp.concatenate(
        [maps[2 * c] * real - maps[2 * c + 1] * imag for c in range(count)], axis=0
    )
    prod_imag = jnp.concatenate(
        [maps[2 * c] * imag + maps[2 * c + 1] * real for c in range(count)], axis=0
    )
    re, im = complex_product(by_right, prod_real, prod_imag, t)
    return complex_product(by_left, to_lanes(re, count), to_lanes(im, count), t)


def adjoint(re, im, maps, count, tables):
    t = pick(tables, True)
    re, im = complex_product(by_left, re, im, t)
    re, im = complex_product(by_right, to_rows(re, count), to_rows(im, count), t)
    rows = re.shape[0] // count
    out_real = out_imag = 0.0
    for c in range(count):
        a, b = re[c * rows : (c + 1) * rows], im[c * rows : (c + 1) * rows]
        sr, si = maps[2 * c], maps[2 * c + 1]
        out_real = out_real + (sr * a + si * b)
        out_imag = out_imag + (sr * b - si * a)
    return out_real, out_imag


def total(values):
    return jnp.sum(jnp.sum(values, axis=0, keepdims=True), axis=1, keepdims=True)


def inner(first, second):
    return total(first[0] * second[0] + first[1] * second[1])


def normal(real, imag, maps, count, tables, wt, spec, part_ref, keep):
    re, im = forward(real, imag, maps, count, tables)
    spec[0], spec[1] = re, im
    keep.start()
    wide = jnp.concatenate([wt] * count, axis=1)
    part_ref[0], part_ref[1] = adjoint(re * wide, im * wide, maps, count, tables)
    keep.wait()


def block_of(turn, half, column, blocks):
    if turn < blocks // 2:
        return turn ^ half ^ (2 * column), column
    return (turn - blocks // 2) ^ half ^ (2 - 2 * column), 1 - column


def block_row(turn, info, blocks, extent):
    column, half = info[0], info[2]
    pair = lax.bitwise_xor(jnp.int32(turn % (blocks // 2)), half)
    if turn < blocks // 2:
        pair = lax.bitwise_xor(pair, 2 * column)
    else:
        pair = lax.bitwise_xor(pair, 2 - 2 * column)
        column = 1 - column
    return pl.multiple_of((pair * 2 + column) * extent, extent)


def at_home(kernel):
    def guarded(*refs):
        @pl.when(refs[0][1] == 1)
        def _():
            kernel(*refs)

    return guarded


def first_kernel(blocks, planes, info, steep_ref, *refs):
    messages, refs = refs[:blocks], refs[blocks:]
    table_ref, maps, image, wt_ref, spec_ref, part_ref, odds, tables, spec, sems = refs
    keep = pltpu.make_async_copy(spec, spec_ref, sems.at[3, 1])
    load = pltpu.make_async_copy(table_ref, tables, sems.at[3, 0])
    extent = messages[0].shape[1]
    copies = []
    for k, msg in enumerate(messages):
        rows = pl.ds(block_row(k, info, blocks, extent), extent)
        copies += [
            pltpu.make_async_copy(msg.at[:planes], maps.at[:, rows], sems.at[0, k]),
            pltpu.make_async_copy(msg.at[pl.ds(planes, 2)], image.at[:, rows], sems.at[1, k]),
            pltpu.make_async_copy(msg.at[planes + 2], odds.at[rows], sems.at[2, k]),
        ]
    for copy in (*copies, load):
        copy.start()
    for copy in (*copies, load):
        copy.wait()
    wt = jax.nn.sigmoid(steep_ref[0] * odds[...]).T
    wt_ref[...] = wt
    normal(image[0], image[1], maps, planes // 2, tables, wt, spec, part_ref, keep)


def second_kernel(info, image, part, other, maps, wt_ref, table_ref, *refs):
    residual_ref, dir_ref, sc_ref, spec_ref, part_ref, tables, spec, sems = refs
    load = pltpu.make_async_copy(table_ref, tables, sems.at[0])
    keep = pltpu.make_async_copy(spec, spec_ref, sems.at[1])
    load.start()
    u = (image[0], image[1])
    q = tuple(part[i] + other[i] + DAMPING * u[i] for i in range(2))
    norm = inner(u, u)
    alpha = norm / inner(u, q)
    r = tuple(u[i] - alpha * q[i] for i in range(2))
    norm_next = inner(r, r)
    p = tuple(r[i] + (norm_next / norm) * u[i] for i in range(2))
    for i in range(2):
        residual_ref[i] = r[i]
        dir_ref[i] = p[i]
    sc_ref[0] = jnp.broadcast_to(alpha, sc_ref.shape[1:])
    sc_ref[1] = jnp.broadcast_to(norm_next, sc_ref.shape[1:])
    load.wait()
    normal(p[0], p[1], maps, maps.shape[0] // 2, tables, wt_ref[...], spec, part_ref, keep)


def third_kernel(blocks, planes, info, image, res_ref, dir_ref, sc_in, part, other, maps,
                 wt_ref, spec0_ref, spec1_ref, *refs):
    messages, refs = refs[:blocks], refs[blocks:]
    table_ref, sol_ref, p_ref, sc_ref, out_ref, data, recon, spec0, spec1, tables, sems = refs
    load = pltpu.make_async_copy(table_ref, tables, sems.at[2, 2])
    load.start()
    extent = messages[0].shape[1]
    copies = []
    for k, msg in enumerate(messages):
        rows = pl.ds(block_row(k, info, blocks, extent), extent)
        copies += [
            pltpu.make_async_copy(msg.at[pl.ds(planes, 2)], recon.at[:, rows], sems.at[1, k]),
            pltpu.make_async_copy(msg.at[:planes], data.at[:, rows], sems.at[0, k]),
        ]
    copies += [
        pltpu.make_async_copy(spec0_ref, spec0, sems.at[2, 0]),
        pltpu.make_async_copy(spec1_ref, spec1, sems.at[2, 1]),
    ]
    for copy in copies:
        copy.start()
    count = planes // 2
    n = image.shape[1]
    alpha0, norm = sc_in[0, :1, :1], sc_in[1, :1, :1]
    p = (dir_ref[0], dir_ref[1])
    q = tuple(part[i] + other[i] + DAMPING * p[i] for i in range(2))
    alpha1 = norm / inner(p, q)
    r = tuple(res_ref[i] - alpha1 * q[i] for i in range(2))
    norm_next = inner(r, r)
    for i in range(2):
        sol_ref[i] = alpha0 * image[i] + alpha1 * p[i]
    p = tuple(r[i] + (norm_next / norm) * p[i] for i in range(2))
    p_ref[0], p_ref[1] = p
    load.wait()
    re, im = forward(p[0], p[1], maps, count, tables)
    wide = jnp.concatenate([wt_ref[...]] * count, axis=1)
    energy = total(wide * (re * re + im * im))
    sc_ref[0] = jnp.broadcast_to(norm_next, sc_ref.shape[1:])
    sc_ref[1] = jnp.broadcast_to(inner(p, p), sc_ref.shape[1:])
    for copy in copies:
        copy.wait()
    est_re, est_im = forward(recon[0], recon[1], maps, count, tables)
    known = last = 0.0
    for c in range(count):
        s = slice(c * n, (c + 1) * n)
        diff_re = data[2 * c].T - est_re[:, s]
        diff_im = data[2 * c + 1].T - est_im[:, s]
        sol_re = alpha0 * spec0[0, :, s] + alpha1 * spec1[0, :, s]
        sol_im = alpha0 * spec0[1, :, s] + alpha1 * spec1[1, :, s]
        known = known + (sol_re * diff_re + sol_im * diff_im)
        last = last + (re[:, s] * diff_re + im[:, s] * diff_im)
    out_ref[:n] = known
    out_ref[n : 2 * n] = last
    out_ref[2 * n :] = jnp.broadcast_to(energy, (out_ref.shape[0] - 2 * n, n))


def fourth_kernel(info, mine, other, sol, p_ref, sc, *refs):
    outs, terms = refs[:-1], refs[-1]
    half = info[2]
    n = sol.shape[1]
    extent = outs[0].shape[1]
    energy = mine[2 * n :, :][:1, :1] + other[2 * n :, :][:1, :1] + DAMPING * sc[1, :1, :1]
    alpha = sc[0, :1, :1] / energy
    terms[...] = (
        (mine[:n] + other[:n]) + alpha * (mine[n : 2 * n] + other[n : 2 * n])
    ).T
    lower, upper = (scatter_order(i, 2 * len(outs)) for i in range(2))
    for k, out in enumerate(outs):
        block = jnp.where(half == 1, len(outs) + upper[k], lower[k])
        rows = pl.ds(pl.multiple_of(block * extent, extent), extent)
        out[0] = sol[0, rows] + alpha * p_ref[0, rows]
        out[1] = sol[1, rows] + alpha * p_ref[1, rows]
        out[2] = terms[rows]


def call(*args, **kwargs):
    def run(*operands):
        return pl.pallas_call(*args, compiler_params=PARAMS, **kwargs)(*operands)

    return run


VMEM = pl.BlockSpec(memory_space=pltpu.VMEM)
SMEM = pl.BlockSpec(memory_space=pltpu.SMEM)
HBM = pl.BlockSpec(memory_space=pltpu.HBM)
PARAMS = pltpu.CompilerParams(vmem_limit_bytes=20 << 20)


def in_hbm(values):
    return pltpu.with_memory_space_constraint(values, pltpu.HBM)


def shape(*dims):
    return jax.ShapeDtypeStruct(dims, F32)


def home_row(piece, blocks):
    first = blocks // 4
    return first if piece % 2 == 0 else blocks - 1 - first


def detour(piece, blocks):
    return (blocks // 2 - 1) * (piece % 2)


def carrier(piece, pair, turn, blocks):
    return (piece ^ (1 - turn % 2)) * blocks + pair * 2 + piece % 2


def gather_pairs(turn, pieces, blocks, moved):
    pairs = []
    for piece in range(pieces):
        for half in range(2):
            pair, column = block_of(turn, half, piece % 2, blocks)
            source = piece * blocks + pair * 2 + column
            if column != piece % 2 and moved(piece, pair):
                source = carrier(piece, pair, turn, blocks)
            target = (piece - piece % 2 + half) * blocks + home_row(piece, blocks)
            pairs.append((source, target))
    return pairs


def move_pairs(turn, pieces, blocks, moved):
    pairs = []
    for piece in range(pieces):
        for pair in range(blocks // 2):
            if moved(piece, pair):
                source = piece * blocks + pair * 2 + 1 - piece % 2
                pairs.append((source, carrier(piece, pair, turn, blocks)))
    return pairs


def scatter_order(half, blocks):
    last = home_row(half, blocks) - half * (blocks // 2)
    return [i for i in range(blocks // 2) if i != last] + [last]


def scatter_pairs(turn, pieces, blocks):
    pairs = []
    for piece in range(pieces):
        for half in range(2):
            source = (piece - piece % 2 + half) * blocks + home_row(piece, blocks)
            block = scatter_order(half, blocks)[turn] + half * (blocks // 2)
            pairs.append((source, piece * blocks + block))
    return pairs


def steps(
    upstream_loss_derivative,
    estimated_slice_image,
    receiver_profile_maps,
    measured_fourier_data,
    acquisition_choice_odds,
    sigmoid_steepness,
):
    blocks = lax.axis_size("rows")
    pieces = lax.axis_size("cuts")
    row = lax.axis_index("rows")
    half = lax.rem(lax.axis_index("cuts"), 2)
    column = (row == home_row(1, blocks)).astype(jnp.int32)
    home = column + (row == home_row(0, blocks)).astype(jnp.int32)
    info = jnp.stack([column, home, half]).astype(jnp.int32)
    odd = lax.rem(row // 2, 2)
    extent = upstream_loss_derivative.shape[3]
    n = upstream_loss_derivative.shape[4]
    coils = receiver_profile_maps.shape[1]
    planes = coils
    count = coils // 2
    tables = jnp.asarray(np.stack(dft_tables(n)))
    table_space = pltpu.VMEM(tables.shape, BF16)
    spec_space = pltpu.VMEM((2, n, count * n), F32)
    swap = [(i, i ^ 1) for i in range(pieces)]

    maps = receiver_profile_maps.reshape(2, planes, extent, n)
    data = measured_fourier_data.reshape(2, planes, extent, n)
    upstream = upstream_loss_derivative.reshape(2, extent, n)
    recon = estimated_slice_image.reshape(2, extent, n)
    take = lambda values, i: lax.dynamic_index_in_dim(values, i, 0, keepdims=False)

    def build(values, *more):
        sends = [jnp.concatenate([take(values, i), *more], axis=0) for i in (odd, 1 - odd)]
        return lax.optimization_barrier(sends)

    def ends(piece, pair):
        return pair == detour(piece, blocks)

    def remote(piece, pair):
        return all(pair != home_row(i, blocks) // 2 for i in range(2))

    def move(sends, moved):
        return [
            lax.ppermute(send, BOTH, move_pairs(i, pieces, blocks, moved))
            for i, send in enumerate(sends)
        ]

    device = lax.axis_index("cuts") * blocks + row

    def passing(sends, turns, moved, carried=None):
        out = []
        for i in range(2):
            groups = []
            for k in [k for k in turns if k % 2 == i]:
                pairs = gather_pairs(k, pieces, blocks, moved)
                carry = {t for _, t in move_pairs(k, pieces, blocks, moved)} if carried else set()
                own = {s for s, _ in gather_pairs(k, pieces, blocks, lambda *_: False)}
                sources = {s for s, _ in pairs}
                passed, direct = (sources & carry) - (sources & own), sources & own
                for group in groups:
                    if not (group[1] | passed) & (group[2] | direct):
                        break
                else:
                    group = [[], set(), set()]
                    groups.append(group)
                group[0].append((k, pairs))
                group[1] |= passed
                group[2] |= direct
            for rounds, passed, _ in groups:
                send = sends[i]
                if passed:
                    here = functools.reduce(lambda x, t: x | (device == t), sorted(passed), False)
                    send = jnp.where(here, carried[i], send)
                out.append((send, rounds))
        return out

    def gather(sends, turns, moved, carried=None):
        got = {}
        for send, rounds in passing(sends, turns, moved, carried):
            got |= {k: lax.ppermute(send, BOTH, pairs) for k, pairs in rounds}
        return got

    turns = blocks // 2
    near, far = range(turns), range(turns, blocks)
    late = sorted({turns + 2, turns + 3, blocks - 2, blocks - 1})
    sends = build(maps, upstream, acquisition_choice_odds)
    first = gather(sends, [k for k in far if k not in late], ends)
    carried = move(sends, ends)
    first |= gather(sends, near, ends)
    first |= gather(sends, late, ends, carried)
    first = [in_hbm(first[k]) for k in range(blocks)]
    sends = build(data, recon)
    carried = move(sends, remote)
    second = gather(sends, near[2:], remote)
    sends = passing(sends, near[:2], remote) + passing(sends, far, remote, carried)
    ready = lax.optimization_barrier((info, *[send for send, _ in sends]))
    info, sends = ready[0], [(send, rounds) for send, (_, rounds) in zip(ready[1:], sends)]
    for send, rounds in sends:
        second |= {k: lax.ppermute(send, BOTH, pairs) for k, pairs in rounds}
    second = [second[k] for k in range(blocks)]

    image, spectrum = shape(2, n, n), shape(2, n, count * n)
    scalars = shape(2, 8, 128)
    stacked = shape(planes, n, n)
    maps_full, u, wt, spec0, part0 = call(
        at_home(functools.partial(first_kernel, blocks, planes)),
        in_specs=[SMEM, SMEM] + [HBM] * (blocks + 1),
        out_specs=[VMEM] * 3 + [HBM] + [VMEM],
        out_shape=[stacked, image, shape(n, n), spectrum, image],
        scratch_shapes=[
            pltpu.VMEM((n, n), F32),
            table_space,
            spec_space,
            pltpu.SemaphoreType.DMA((4, blocks)),
        ],
    )(info, sigmoid_steepness, *first, tables)
    other0 = lax.ppermute(part0, "cuts", swap)
    res1, dir1, sc1, spec1, part1 = call(
        at_home(second_kernel),
        in_specs=[SMEM] + [VMEM] * 5 + [HBM],
        out_specs=[VMEM] * 3 + [HBM] + [VMEM],
        out_shape=[image, image, scalars, spectrum, image],
        scratch_shapes=[table_space, spec_space, pltpu.SemaphoreType.DMA((2,))],
    )(info, u, part0, other0, maps_full, wt, tables)
    other1 = lax.ppermute(part1, "cuts", swap)
    sol2, dir2, sc2, mine = call(
        at_home(functools.partial(third_kernel, blocks, planes)),
        in_specs=[SMEM] + [VMEM] * 8 + [HBM] * (blocks + 3),
        out_specs=[VMEM] * 4,
        out_shape=[image, image, scalars, shape(2 * n + 8, n)],
        scratch_shapes=[
            pltpu.VMEM((planes, n, n), F32),
            pltpu.VMEM((2, n, n), F32),
            spec_space,
            spec_space,
            table_space,
            pltpu.SemaphoreType.DMA((3, blocks)),
        ],
    )(info, u, res1, dir1, sc1, part1, other1, maps_full, wt, spec0, spec1, *second, tables)
    other = lax.ppermute(mine, "cuts", swap)
    outs = call(
        at_home(fourth_kernel),
        in_specs=[SMEM] + [VMEM] * 5,
        out_specs=[VMEM] * turns,
        out_shape=[shape(3, extent, n)] * turns,
        scratch_shapes=[pltpu.VMEM((n, n), F32)],
    )(info, mine, other, sol2, dir2, sc2)
    parts = [
        lax.ppermute(outs[k], BOTH, scatter_pairs(k, pieces, blocks)) for k in range(turns)
    ]
    whole = parts[0]
    for part in parts[1:]:
        whole = whole + part
    term = whole[2]
    step = 1
    while step < pieces:
        term = term + lax.ppermute(term, "cuts", [(i, i ^ step) for i in range(pieces)])
        step *= 2
    steep = sigmoid_steepness[0]
    weights = jax.nn.sigmoid(steep * acquisition_choice_odds)
    slices = upstream_loss_derivative.shape[0] * pieces
    gradient = steep * weights * (1.0 - weights) * term[None] / slices
    return whole[:2].reshape(upstream_loss_derivative.shape), gradient


def solution(mesh):
    return jax.shard_map(
        steps,
        mesh=mesh,
        in_specs=(
            P("cuts", None, None, "rows", None),
            P("cuts", None, None, "rows", None),
            P("cuts", None, None, "rows", None),
            P("cuts", None, None, None, "rows", None),
            P(None, "rows", None),
            P(),
        ),
        out_specs=(P("cuts", None, None, "rows", None), P(None, "rows", None)),
        check_vma=False,
    )
```
